768 devices in a mesh: dp: 96 (over y, z), tensor: 8 (over x, core).
Axes of the slice: x: 4, y: 8, z: 12, core: 2. Of those that a mesh axis runs over, the one named last changes fastest.
Arguments:
- queries: bfloat16 [49152, 3072], P('dp', 'tensor'), may hold values from -6 to 6
- keys: bfloat16 [49152, 3072], P('dp', 'tensor'), may hold values from -6 to 6
- values: bfloat16 [49152, 3072], P('dp', 'tensor'), may hold values from -6 to 6
- out_grad: bfloat16 [49152, 3072], P('dp', 'tensor'), may hold values from -6 to 6
- lengths: int32 [384], replicated, may hold values from 1 to 512, 49152 in all
Outputs:
- attn_out: bfloat16 [49152, 3072], P('dp', 'tensor')
- query_grad: bfloat16 [49152, 3072], P('dp', 'tensor')
- key_grad: bfloat16 [49152, 3072], P('dp', 'tensor')
- value_grad: bfloat16 [49152, 3072], P('dp', 'tensor')
The draws below stay inside these ranges and needn't reach their ends.
Inputs may be any that keep to these rules, and one draw needn't show every extreme that they name: `lengths`: 384 token counts that sum to 49152, at least one image 512 long.
All inputs are finite; a program needn't handle non-finite values.
Results may differ from the reference program's by a relative error of at most 0.012.
Values may be sent and summed in bfloat16 or wider, within the bound.
A program may use at most 64 MiB of HBM per device.

```python
import math
import jax
import jax.numpy as jnp
import numpy as np
from jax import lax

HEADS = 24
HEAD_DIM = 128
TOK_DEV = 512
MOST = 512
IMAGES = 384
TOKENS = 49152
N_DP = 96


def draw_queries(key, part):
    shape = (TOKENS, HEADS * HEAD_DIM)
    return jnp.clip(jax.random.normal(jax.random.fold_in(key, 21), shape, jnp.float32), -6.0, 6.0).astype(jnp.bfloat16)


def draw_keys(key, part):
    shape = (TOKENS, HEADS * HEAD_DIM)
    return jnp.clip(jax.random.normal(jax.random.fold_in(key, 31), shape, jnp.float32), -6.0, 6.0).astype(jnp.bfloat16)


def levels(key, extent, split, smallest, top_value):
    factor_of = 1.0
    for dim, blocks in split:
        steps = jax.random.uniform(jax.random.fold_in(jax.random.fold_in(key, 6), dim), (blocks,), jnp.float32, smallest / len(split), top_value / len(split))
        factor_of = factor_of * jnp.repeat(jnp.exp(steps), extent[dim] // blocks).reshape((-1,) + (1,) * (len(extent) - 1 - dim))
    return factor_of


def length_profile(amount, total, limit, skew):
    weights = [(1 << 20) // math.isqrt(rank ** skew) + 1 for rank in range(2, amount + 1)]
    rest, counts = total - limit - (amount - 1), [1] * (amount - 1)
    while rest > 0:
        free = [i for i in range(amount - 1) if counts[i] < limit]
        pool, left = sum([weights[i] for i in free]), rest
        for i in free:
            extra = min(limit - counts[i], max(1, left * weights[i] // pool), rest)
            counts[i] = counts[i] + extra
            rest = rest - extra
    return np.array([limit] + counts)


def ragged(rng, number_of, total, most, slope):
    if number_of == 2:
        one = jax.random.randint(rng, (), max(1, total - most), min(most, total - 1) + 1)
        return jnp.stack([one, total - one])
    sizes = jnp.asarray(length_profile(number_of, total, most, slope), jnp.int32)
    couples = (number_of - 1) // 2
    donor, taker = sizes[1:1 + 2 * couples:2], sizes[2:2 + 2 * couples:2]
    room = jnp.minimum(donor - 1, most - taker)
    shifted = jax.random.randint(jax.random.fold_in(rng, 1), (couples,), 0, 1 << 20) % (room + 1)
    sizes = sizes.at[1:1 + 2 * couples:2].set(donor - shifted).at[2:2 + 2 * couples:2].set(taker + shifted)
    return sizes[jax.random.permutation(jax.random.fold_in(rng, 2), number_of)]


def centred(stream_key, extent, scale, bound, shards=(), kind=jnp.bfloat16):
    factor_of = levels(stream_key, extent, shards, -0.22, 0.18) if shards else 1.0
    values = jax.random.normal(stream_key, extent, jnp.float32) * scale * factor_of
    return jnp.minimum(jnp.maximum(values, -bound), bound).astype(kind)


def setup_inputs(seed: int = 0) -> dict:
    arg_keys = jax.random.split(jax.random.key(seed), 6)
    queries = draw_queries(jax.random.fold_in(arg_keys[5], 71), 0)
    keys = draw_keys(jax.random.fold_in(arg_keys[5], 71), 0)
    values = centred(arg_keys[2], (TOKENS, HEADS * HEAD_DIM), 1.0, 6.0, ((0, 96), (1, 8)))
    out_grad = centred(arg_keys[3], (TOKENS, HEADS * HEAD_DIM), 1.0, 6.0, ((0, 96), (1, 8)))
    lengths = ragged(arg_keys[4], IMAGES, TOKENS, MOST, 2).astype(jnp.int32)
    return {"queries": queries, "keys": keys, "values": values, "out_grad": out_grad, "lengths": lengths}


def image_masks(lengths, first_row, count, total_rows, span):
    ends = jnp.cumsum(lengths).astype(jnp.int32)
    starts = ends - lengths.astype(jnp.int32)
    positions = first_row + jnp.arange(count, dtype=jnp.int32)
    begin = lax.optimization_barrier(jnp.max(jnp.where(starts[None, :] <= positions[:, None], starts[None, :], -1), axis=1))
    valid = positions < total_rows
    owned_rows = valid & (begin >= first_row) & (begin < first_row + span)
    window_mask = owned_rows[:, None] & valid[None, :] & (begin[:, None] == begin[None, :])
    return (window_mask, owned_rows)

def head_attention(operands, window_mask, owned_rows, factor):
    query_head, key_head, value_head, grad_head = operands
    scores = jnp.dot(query_head, key_head.T, preferred_element_type=jnp.float32) * factor
    scores = jnp.where(window_mask, scores, -1e+30)
    top_score = lax.optimization_barrier(jnp.max(scores, axis=1, keepdims=True))
    weights = jnp.where(window_mask, jnp.exp(scores - top_score), 0.0)
    totals = lax.optimization_barrier(jnp.sum(weights, axis=1, keepdims=True))
    totals = jnp.where(owned_rows[:, None], totals, 1.0)
    probs = weights / totals
    probs_low = probs.astype(jnp.bfloat16)
    result = jnp.dot(probs_low, value_head, preferred_element_type=jnp.float32).astype(jnp.bfloat16)
    grad_probs = jnp.dot(grad_head, value_head.T, preferred_element_type=jnp.float32)
    centre = lax.optimization_barrier(jnp.sum(grad_head.astype(jnp.float32) * result.astype(jnp.float32), axis=1, keepdims=True))
    grad_scores = (probs * (grad_probs - centre)).astype(jnp.bfloat16)
    grad_query = (jnp.dot(grad_scores, key_head, preferred_element_type=jnp.float32) * factor).astype(jnp.bfloat16)
    grad_key = (jnp.dot(grad_scores.T, query_head, preferred_element_type=jnp.float32) * factor).astype(jnp.bfloat16)
    grad_value = jnp.dot(probs_low.T, grad_head, preferred_element_type=jnp.float32).astype(jnp.bfloat16)
    return (result, grad_query, grad_key, grad_value)

def all_heads(window, window_mask, owned_rows):
    count = window[0].shape[0]
    factor = 1.0 / math.sqrt(HEAD_DIM)

    def split_heads(block):
        return block.reshape(count, -1, HEAD_DIM).transpose(1, 0, 2)
    stacked = (split_heads(window[0]), split_heads(window[1]), split_heads(window[2]), split_heads(window[3]))

    def one_head(operands):
        return head_attention(operands, window_mask, owned_rows, factor)
    outputs = lax.map(one_head, stacked)
    return tuple((output.transpose(1, 0, 2).reshape(count, -1) for output in outputs))

def reference(queries, keys, values, out_grad, lengths):
    rows = TOK_DEV
    padded = tuple((jnp.concatenate([array, jnp.zeros((rows, array.shape[1]), array.dtype)], axis=0) for array in (queries, keys, values, out_grad)))

    def window_results(index):
        first_row = (index * rows).astype(jnp.int32)
        window = tuple((lax.dynamic_slice_in_dim(array, first_row, 2 * rows, 0) for array in padded))
        window_mask, owned_rows = image_masks(lengths, first_row, 2 * rows, TOKENS, rows)
        return all_heads(window, window_mask, owned_rows)
    results = lax.map(window_results, jnp.arange(N_DP, dtype=jnp.int32))
    combined = []
    for stacked in results:
        own_part = stacked[:, :rows]
        spill = stacked[:, rows:]
        moved = jnp.concatenate([jnp.zeros_like(spill[:1]), spill[:-1]], axis=0)
        combined.append((own_part + moved).reshape(TOKENS, -1))
    return (combined[0], combined[1], combined[2], combined[3])
```

```python
import functools
import math

import jax
import jax.numpy as jnp
from jax import lax
from jax.experimental import pallas as pl
from jax.experimental.pallas import tpu as pltpu
from jax.sharding import PartitionSpec as P

D = 128
HALO = 256
BLK = 256
MESH = pl.DeviceIdType.MESH
LOG2E = 1.4426950408889634


def row_tables(len_ref, first, total, halo, rows):
    lens = len_ref[...]
    groups = lens.shape[0]
    upper = (
        lax.broadcasted_iota(jnp.int32, (128, 128), 0)
        <= lax.broadcasted_iota(jnp.int32, (128, 128), 1)
    ).astype(jnp.float32).astype(jnp.bfloat16)
    high = (lens >> 4).astype(jnp.float32).astype(jnp.bfloat16)
    low = (lens & 15).astype(jnp.float32).astype(jnp.bfloat16)
    within = 16.0 * jnp.dot(high, upper, preferred_element_type=jnp.float32) + jnp.dot(
        low, upper, preferred_element_type=jnp.float32
    )
    ends, base = [], jnp.zeros((1, 1), jnp.float32)
    for g in range(groups):
        ends.append(within[g : g + 1, :] + base)
        base = base + within[g : g + 1, 127:128]
    count = rows + 2 * halo
    pos = (
        first - halo + lax.broadcasted_iota(jnp.int32, (count, 128), 0)
    ).astype(jnp.float32)
    begin = jnp.full((count, 128), 0.0, jnp.float32)
    end = jnp.full((count, 128), 1e9, jnp.float32)
    for e in ends:
        past = e <= pos
        begin = jnp.maximum(begin, jnp.where(past, e, 0.0))
        end = jnp.minimum(end, jnp.where(past, 1e9, e))
    begin = jnp.max(begin, axis=1, keepdims=True)
    end = jnp.min(end, axis=1, keepdims=True)
    begin = jnp.where(pos[:, :1] < 0.0, -1.0, begin)
    return begin, end


def kernel(
    n_dp, rows, heads,
    q_hbm, k_hbm, v_hbm, g_hbm, len_ref,
    o_ref, dq_ref, dk_ref, dv_ref,
    win, res, from_left, from_right, idc, idr, qt, gt, p_s, ds_s,
    own_sem, send1, recv1, send2, recv2,
):
    halo, d = HALO, D
    count = rows + 2 * halo
    me = lax.axis_index("dp")
    ten = lax.axis_index("tensor")
    right = lax.rem(me + 1, n_dp)
    left = lax.rem(me + n_dp - 1, n_dp)
    srcs = (q_hbm, k_hbm, v_hbm, g_hbm)
    outs = (o_ref, dq_ref, dk_ref, dv_ref)

    def out_copy(x, h, way):
        cols = pl.ds(h * d, d)
        if way == 0:
            src, dst, who = pl.ds(rows - halo, halo), pl.ds(0, halo), right
        else:
            src, dst, who = pl.ds(0, halo), pl.ds(halo + rows, halo), left
        return pltpu.make_async_remote_copy(
            src_ref=srcs[x].at[src, cols],
            dst_ref=win.at[x, h, dst, :],
            send_sem=send1.at[h, x, way],
            recv_sem=recv1.at[h, x, way],
            device_id=(who, ten),
            device_id_type=MESH,
        )

    def back_copy(h, way):
        if way == 0:
            src, dst, who = res.at[:, h, pl.ds(halo + rows, halo), :], from_left.at[h], right
        else:
            src, dst, who = res.at[:, h, pl.ds(0, halo), :], from_right.at[h], left
        return pltpu.make_async_remote_copy(
            src_ref=src,
            dst_ref=dst,
            send_sem=send2.at[h, way],
            recv_sem=recv2.at[h, way],
            device_id=(who, ten),
            device_id_type=MESH,
        )

    def own_copy(x, h):
        return pltpu.make_async_copy(
            srcs[x].at[:, pl.ds(h * d, d)], win.at[x, h, pl.ds(halo, rows), :], own_sem.at[h, x]
        )

    barrier = pltpu.get_barrier_semaphore()
    for who in (left, right):
        pl.semaphore_signal(barrier, inc=1, device_id=(who, ten), device_id_type=MESH)
    pl.semaphore_wait(barrier, 2)

    for h in range(heads):
        for x in range(4):
            for way in range(2):
                out_copy(x, h, way).start()
    for h in range(heads):
        for x in range(4):
            own_copy(x, h).start()

    first = me * rows
    begin, end = row_tables(len_ref, first, rows * n_dp, halo, rows)
    idc[...] = jnp.broadcast_to(begin, (count, d))
    idr[...] = jnp.transpose(jnp.broadcast_to(begin, (count, d)))[:8, :]
    edge_l = first.astype(jnp.float32)
    edge_r = (first + rows).astype(jnp.float32)
    b_l, e_l = begin[halo : 2 * halo], end[halo : 2 * halo]
    gone_l = (b_l < edge_l) & (e_l - edge_l <= edge_l - b_l)
    b_r, e_r = begin[rows : rows + halo], end[rows : rows + halo]
    gone_r = (e_r > edge_r) & (e_r - edge_r > edge_r - b_r)
    factor = 1.0 / math.sqrt(d)
    nblk = count // BLK

    def one_head(h, carry):
        for x in range(4):
            own_copy(x, h).wait()
            for way in range(2):
                out_copy(x, h, way).wait_recv()
        qt[...] = jnp.transpose(win[0, h])
        gt[...] = jnp.transpose(win[3, h])
        for i in range(nblk):
            rs = slice(i * BLK, (i + 1) * BLK)
            ks = slice(max(0, i - 2) * BLK, min(nblk, i + 3) * BLK)
            qb, gb = win[0, h, rs, :], win[3, h, rs, :]
            kb, vb = win[1, h, ks, :], win[2, h, ks, :]
            s = lax.dot_general(
                qb, kb, (((1,), (1,)), ((), ())), preferred_element_type=jnp.float32
            ) * (factor * LOG2E)
            s = jnp.where(idc[rs, :1] == idr[:1, ks], s, -1e30)
            top = jnp.max(s, axis=1, keepdims=True)
            w = jnp.exp2(s - top)
            total = jnp.sum(w, axis=1, keepdims=True)
            probs = w * (1.0 / total)
            low = probs.astype(jnp.bfloat16)
            o = jnp.dot(low, vb, preferred_element_type=jnp.float32).astype(jnp.bfloat16)
            res[0, h, rs, :] = o
            p_s[rs, ks] = low
            gp = lax.dot_general(
                gb, vb, (((1,), (1,)), ((), ())), preferred_element_type=jnp.float32
            )
            centre = jnp.sum(
                gb.astype(jnp.float32) * o.astype(jnp.float32), axis=1, keepdims=True
            )
            ds = (probs * (gp - centre)).astype(jnp.bfloat16)
            ds_s[rs, ks] = ds
            res[1, h, rs, :] = (
                jnp.dot(ds, kb, preferred_element_type=jnp.float32) * factor
            ).astype(jnp.bfloat16)
        for j in range(nblk):
            js = slice(j * BLK, (j + 1) * BLK)
            rs = slice(max(0, j - 2) * BLK, min(nblk, j + 3) * BLK)
            dkt = jnp.dot(qt[:, rs], ds_s[rs, js], preferred_element_type=jnp.float32)
            dvt = jnp.dot(gt[:, rs], p_s[rs, js], preferred_element_type=jnp.float32)
            res[2, h, js, :] = jnp.transpose(dkt * factor).astype(jnp.bfloat16)
            res[3, h, js, :] = jnp.transpose(dvt).astype(jnp.bfloat16)
        for way in range(2):
            back_copy(h, way).start()
        return carry

    lax.fori_loop(0, heads, one_head, 0)

    for h in range(heads):
        for way in range(2):
            back_copy(h, way).wait_recv()
        cols = slice(h * d, (h + 1) * d)
        for x in range(4):
            outs[x][0:halo, cols] = jnp.where(
                gone_l, from_left[h, x], res[x, h, halo : 2 * halo, :]
            )
            outs[x][rows - halo : rows, cols] = jnp.where(
                gone_r, from_right[h, x], res[x, h, rows : rows + halo, :]
            )
    for h in range(heads):
        for way in range(2):
            back_copy(h, way).wait_send()
            for x in range(4):
                out_copy(x, h, way).wait_send()


def body(queries, keys, values, out_grad, lengths):
    rows, width = queries.shape
    heads = width // D
    n_dp = lax.axis_size("dp")
    count = rows + 2 * HALO
    out = jax.ShapeDtypeStruct((rows, width), jnp.bfloat16)
    bf = jnp.bfloat16
    pairs = count * count * heads
    return pl.pallas_call(
        functools.partial(kernel, n_dp, rows, heads),
        out_shape=(out,) * 4,
        in_specs=[pl.BlockSpec(memory_space=pl.ANY)] * 4 + [pl.BlockSpec(memory_space=pltpu.VMEM)],
        out_specs=(pl.BlockSpec(memory_space=pltpu.VMEM),) * 4,
        scratch_shapes=[
            pltpu.VMEM((4, heads, count, D), bf),
            pltpu.VMEM((4, heads, count, D), bf),
            pltpu.VMEM((heads, 4, HALO, D), bf),
            pltpu.VMEM((heads, 4, HALO, D), bf),
            pltpu.VMEM((count, D), jnp.float32),
            pltpu.VMEM((8, count), jnp.float32),
            pltpu.VMEM((D, count), bf),
            pltpu.VMEM((D, count), bf),
            pltpu.VMEM((count, count), bf),
            pltpu.VMEM((count, count), bf),
            pltpu.SemaphoreType.DMA((heads, 4)),
            pltpu.SemaphoreType.DMA((heads, 4, 2)),
            pltpu.SemaphoreType.DMA((heads, 4, 2)),
            pltpu.SemaphoreType.DMA((heads, 2)),
            pltpu.SemaphoreType.DMA((heads, 2)),
        ],
        compiler_params=pltpu.CompilerParams(
            collective_id=0, has_side_effects=True, vmem_limit_bytes=48 << 20
        ),
        cost_estimate=pl.CostEstimate(
            flops=12 * pairs * D, bytes_accessed=16 * rows * width, transcendentals=pairs
        ),
    )(queries, keys, values, out_grad, lengths.reshape(-1, 128))


def solution(mesh):
    spec = P("dp", "tensor")
    return jax.shard_map(
        body, mesh=mesh, in_specs=(spec,) * 4 + (P(),), out_specs=(spec,) * 4, check_vma=False
    )
```

```python
import functools
import math

import jax
import jax.numpy as jnp
from jax import lax
from jax.experimental import pallas as pl
from jax.experimental.pallas import tpu as pltpu
from jax.sharding import PartitionSpec as P

D = 128
HALO = 256
BLK = 256
MESH = pl.DeviceIdType.MESH
LOG2E = 1.4426950408889634


def row_tables(len_ref, first, total, halo, rows):
    lens = len_ref[...]
    groups = lens.shape[0]
    upper = (
        lax.broadcasted_iota(jnp.int32, (128, 128), 0)
        <= lax.broadcasted_iota(jnp.int32, (128, 128), 1)
    ).astype(jnp.float32).astype(jnp.bfloat16)
    high = (lens >> 4).astype(jnp.float32).astype(jnp.bfloat16)
    low = (lens & 15).astype(jnp.float32).astype(jnp.bfloat16)
    within = 16.0 * jnp.dot(high, upper, preferred_element_type=jnp.float32) + jnp.dot(
        low, upper, preferred_element_type=jnp.float32
    )
    ends, base = [], jnp.zeros((1, 1), jnp.float32)
    for g in range(groups):
        ends.append(within[g : g + 1, :] + base)
        base = base + within[g : g + 1, 127:128]
    count = rows + 2 * halo
    pos = (
        first - halo + lax.broadcasted_iota(jnp.int32, (count, 128), 0)
    ).astype(jnp.float32)
    begin = jnp.full((count, 128), 0.0, jnp.float32)
    end = jnp.full((count, 128), 1e9, jnp.float32)
    for e in ends:
        past = e <= pos
        begin = jnp.maximum(begin, jnp.where(past, e, 0.0))
        end = jnp.minimum(end, jnp.where(past, 1e9, e))
    begin = jnp.max(begin, axis=1, keepdims=True)
    end = jnp.min(end, axis=1, keepdims=True)
    begin = jnp.where(pos[:, :1] < 0.0, -1.0, begin)
    return begin, end


def kernel(
    n_dp, rows, heads,
    q_hbm, k_hbm, v_hbm, g_hbm, len_hbm,
    out_ref,
    win, res, from_left, from_right, idc, idr, qt, gt, p_s, ds_s, len_ref,
    own_sem, len_sem, send1, recv1, send2, recv2,
):
    halo, d = HALO, D
    count = rows + 2 * halo
    me = lax.axis_index("dp")
    ten = lax.axis_index("tensor")
    right = lax.rem(me + 1, n_dp)
    left = lax.rem(me + n_dp - 1, n_dp)
    srcs = (q_hbm, k_hbm, v_hbm, g_hbm)
    outs = tuple(out_ref.at[x] for x in range(4))

    def out_copy(x, h, way):
        cols = pl.ds(h * d, d)
        if way == 0:
            src, dst, who = pl.ds(rows - halo, halo), pl.ds(0, halo), right
        else:
            src, dst, who = pl.ds(0, halo), pl.ds(halo + rows, halo), left
        return pltpu.make_async_remote_copy(
            src_ref=srcs[x].at[src, cols],
            dst_ref=win.at[x, h, dst, :],
            send_sem=send1.at[h, x, way],
            recv_sem=recv1.at[h, x, way],
            device_id=(who, ten),
            device_id_type=MESH,
        )

    def back_copy(h, way):
        if way == 0:
            src, dst, who = res.at[:, h, pl.ds(halo + rows, halo), :], from_left.at[h], right
        else:
            src, dst, who = res.at[:, h, pl.ds(0, halo), :], from_right.at[h], left
        return pltpu.make_async_remote_copy(
            src_ref=src,
            dst_ref=dst,
            send_sem=send2.at[h, way],
            recv_sem=recv2.at[h, way],
            device_id=(who, ten),
            device_id_type=MESH,
        )

    def own_copy(x, h):
        return pltpu.make_async_copy(
            srcs[x].at[:, pl.ds(h * d, d)], win.at[x, h, pl.ds(halo, rows), :], own_sem.at[h, x]
        )

    len_copy = pltpu.make_async_copy(len_hbm, len_ref, len_sem)
    len_copy.start()
    barrier = pltpu.get_barrier_semaphore()
    for who in (left, right):
        pl.semaphore_signal(barrier, inc=1, device_id=(who, ten), device_id_type=MESH)
    pl.semaphore_wait(barrier, 2)

    for h in range(heads):
        for x in range(4):
            for way in range(2):
                out_copy(x, h, way).start()
    for h in range(heads):
        for x in range(4):
            own_copy(x, h).start()

    first = me * rows
    len_copy.wait()
    begin, end = row_tables(len_ref, first, rows * n_dp, halo, rows)
    idc[...] = jnp.broadcast_to(begin, (count, d))
    idr[...] = jnp.transpose(jnp.broadcast_to(begin, (count, d)))[:8, :]
    edge_l = first.astype(jnp.float32)
    edge_r = (first + rows).astype(jnp.float32)
    b_l, e_l = begin[halo : 2 * halo], end[halo : 2 * halo]
    gone_l = (b_l < edge_l) & (e_l - edge_l <= edge_l - b_l)
    b_r, e_r = begin[rows : rows + halo], end[rows : rows + halo]
    gone_r = (e_r > edge_r) & (e_r - edge_r > edge_r - b_r)
    factor = 1.0 / math.sqrt(d)
    nblk = count // BLK

    def one_head(h, carry):
        for x in range(4):
            own_copy(x, h).wait()
            for way in range(2):
                out_copy(x, h, way).wait_recv()
        qt[...] = jnp.transpose(win[0, h])
        gt[...] = jnp.transpose(win[3, h])
        for i in range(nblk):
            rs = slice(i * BLK, (i + 1) * BLK)
            ks = slice(max(0, i - 2) * BLK, min(nblk, i + 3) * BLK)
            qb, gb = win[0, h, rs, :], win[3, h, rs, :]
            kb, vb = win[1, h, ks, :], win[2, h, ks, :]
            s = lax.dot_general(
                qb, kb, (((1,), (1,)), ((), ())), preferred_element_type=jnp.float32
            ) * (factor * LOG2E)
            s = jnp.where(idc[rs, :1] == idr[:1, ks], s, -1e30)
            top = jnp.max(s, axis=1, keepdims=True)
            w = jnp.exp2(s - top)
            total = jnp.sum(w, axis=1, keepdims=True)
            probs = w * (1.0 / total)
            low = probs.astype(jnp.bfloat16)
            o = jnp.dot(low, vb, preferred_element_type=jnp.float32).astype(jnp.bfloat16)
            res[0, h, rs, :] = o
            p_s[rs, ks] = low
            gp = lax.dot_general(
                gb, vb, (((1,), (1,)), ((), ())), preferred_element_type=jnp.float32
            )
            centre = jnp.sum(
                gb.astype(jnp.float32) * o.astype(jnp.float32), axis=1, keepdims=True
            )
            ds = (probs * (gp - centre)).astype(jnp.bfloat16)
            ds_s[rs, ks] = ds
            res[1, h, rs, :] = (
                jnp.dot(ds, kb, preferred_element_type=jnp.float32) * factor
            ).astype(jnp.bfloat16)
        for j in range(nblk):
            js = slice(j * BLK, (j + 1) * BLK)
            rs = slice(max(0, j - 2) * BLK, min(nblk, j + 3) * BLK)
            dkt = jnp.dot(qt[:, rs], ds_s[rs, js], preferred_element_type=jnp.float32)
            dvt = jnp.dot(gt[:, rs], p_s[rs, js], preferred_element_type=jnp.float32)
            res[2, h, js, :] = jnp.transpose(dkt * factor).astype(jnp.bfloat16)
            res[3, h, js, :] = jnp.transpose(dvt).astype(jnp.bfloat16)
        for way in range(2):
            back_copy(h, way).start()
        return carry

    lax.fori_loop(0, heads, one_head, 0)

    for h in range(heads):
        for way in range(2):
            back_copy(h, way).wait_recv()
        cols = slice(h * d, (h + 1) * d)
        for x in range(4):
            outs[x][0:halo, cols] = jnp.where(
                gone_l, from_left[h, x], res[x, h, halo : 2 * halo, :]
            )
            outs[x][rows - halo : rows, cols] = jnp.where(
                gone_r, from_right[h, x], res[x, h, rows : rows + halo, :]
            )
    for h in range(heads):
        for way in range(2):
            back_copy(h, way).wait_send()
            for x in range(4):
                out_copy(x, h, way).wait_send()


def store_kernel(o_in, dq_in, dk_in, dv_in, o, dq, dk, dv, sem):
    pairs = ((o_in, o), (dq_in, dq), (dk_in, dk), (dv_in, dv))
    copies = [pltpu.make_async_copy(a, b, sem.at[i]) for i, (a, b) in enumerate(pairs)]
    for copy in copies:
        copy.start()
    for copy in copies:
        copy.wait()


def body(queries, keys, values, out_grad, lengths):
    rows, width = queries.shape
    heads = width // D
    n_dp = lax.axis_size("dp")
    count = rows + 2 * HALO
    out = jax.ShapeDtypeStruct((rows, width), jnp.bfloat16)
    bf = jnp.bfloat16
    pairs = count * count * heads
    operands = [
        pltpu.with_memory_space_constraint(x, pltpu.MemorySpace.HBM)
        for x in (queries, keys, values, out_grad, lengths.reshape(-1, 128))
    ]
    results = pl.pallas_call(
        functools.partial(kernel, n_dp, rows, heads),
        out_shape=jax.ShapeDtypeStruct((4, rows, width), jnp.bfloat16),
        in_specs=[pl.BlockSpec(memory_space=pltpu.MemorySpace.HBM)] * 5,
        out_specs=pl.BlockSpec(memory_space=pltpu.VMEM),
        scratch_shapes=[
            pltpu.VMEM((4, heads, count, D), bf),
            pltpu.VMEM((4, heads, count, D), bf),
            pltpu.VMEM((heads, 4, HALO, D), bf),
            pltpu.VMEM((heads, 4, HALO, D), bf),
            pltpu.VMEM((count, D), jnp.float32),
            pltpu.VMEM((8, count), jnp.float32),
            pltpu.VMEM((D, count), bf),
            pltpu.VMEM((D, count), bf),
            pltpu.VMEM((count, count), bf),
            pltpu.VMEM((count, count), bf),
            pltpu.VMEM((3, 128), jnp.int32),
            pltpu.SemaphoreType.DMA((heads, 4)),
            pltpu.SemaphoreType.DMA(()),
            pltpu.SemaphoreType.DMA((heads, 4, 2)),
            pltpu.SemaphoreType.DMA((heads, 4, 2)),
            pltpu.SemaphoreType.DMA((heads, 2)),
            pltpu.SemaphoreType.DMA((heads, 2)),
        ],
        compiler_params=pltpu.CompilerParams(
            collective_id=0, has_side_effects=True, vmem_limit_bytes=48 << 20
        ),
        cost_estimate=pl.CostEstimate(
            flops=12 * pairs * D, bytes_accessed=16 * rows * width, transcendentals=pairs
        ),
    )(*operands)
    return tuple(results[x] for x in range(4))


def solution(mesh):
    spec = P("dp", "tensor")
    return jax.shard_map(
        body, mesh=mesh, in_specs=(spec,) * 4 + (P(),), out_specs=(spec,) * 4, check_vma=False
    )
```

```python
import functools
import math

import jax
import jax.numpy as jnp
from jax import lax
from jax.experimental import pallas as pl
from jax.experimental.pallas import tpu as pltpu
from jax.sharding import PartitionSpec as P

D = 128
EDGE = 128
HALO = 384
MESH = pl.DeviceIdType.MESH
LOG2E = 1.4426950408889634
BF = jnp.bfloat16
F32 = jnp.float32


def dot_nt(a, b):
    return lax.dot_general(a, b, (((1,), (1,)), ((), ())), preferred_element_type=F32)


def dot_nn(a, b):
    return jnp.dot(a, b, preferred_element_type=F32)


def row_tables(lens, first, count):
    upper = (
        lax.broadcasted_iota(jnp.int32, (128, 128), 0)
        <= lax.broadcasted_iota(jnp.int32, (128, 128), 1)
    ).astype(F32).astype(BF)
    high = (lens >> 4).astype(F32).astype(BF)
    low = (lens & 15).astype(F32).astype(BF)
    within = 16.0 * dot_nn(high, upper) + dot_nn(low, upper)
    pos = (first - HALO + lax.broadcasted_iota(jnp.int32, (count, 128), 0)).astype(F32)
    begin = jnp.zeros((count, 128), F32)
    end = jnp.full((count, 128), 1e9, F32)
    base = jnp.zeros((1, 1), F32)
    for g in range(lens.shape[0]):
        e = within[g : g + 1, :] + base
        base = base + within[g : g + 1, 127:128]
        past = e <= pos
        begin = jnp.maximum(begin, jnp.where(past, e, 0.0))
        end = jnp.minimum(end, jnp.where(past, 1e9, e))
    begin = jnp.max(begin, axis=1, keepdims=True)
    end = jnp.min(end, axis=1, keepdims=True)
    return jnp.where(pos[:, :1] < 0.0, -1.0, begin), end


def kernel(
    n_dp, rows, heads,
    q_hbm, k_hbm, v_hbm, g_hbm, len_hbm,
    out_ref,
    kv, q_own, g_own, qt, gt, packed, back, from_left, from_right,
    idc, idr, p_s, ds_s, own_kv, len_ref,
    own_sem, len_sem, send1, recv1, send2, recv2,
):
    halo, edge, d = HALO, EDGE, D
    count = rows + 2 * halo
    qrows = rows + 2 * edge
    me = lax.axis_index("dp")
    ten = lax.axis_index("tensor")
    right = lax.rem(me + 1, n_dp)
    left = lax.rem(me + n_dp - 1, n_dp)
    raw = halo - edge

    def remote(src, dst, send, recv, who):
        return pltpu.make_async_remote_copy(
            src_ref=src, dst_ref=dst, send_sem=send, recv_sem=recv,
            device_id=(who, ten), device_id_type=MESH,
        )

    def raw_copy(x, h, way):
        src = pl.ds(rows - raw, raw) if way == 0 else pl.ds(0, raw)
        dst = pl.ds(edge, raw) if way == 0 else pl.ds(halo + rows, raw)
        return remote(
            (k_hbm, v_hbm)[x].at[src, pl.ds(h * d, d)], kv.at[h, x, dst, :],
            send1.at[h, x, way], recv1.at[h, x, way], (right, left)[way],
        )

    def packed_copy(h, way):
        dst = pl.ds(0, edge) if way == 0 else pl.ds(count - edge, edge)
        return remote(
            packed.at[h, way], kv.at[h, :, dst, :],
            send1.at[h, 2, way], recv1.at[h, 2, way], (right, left)[way],
        )

    def back_copy(h, way):
        return remote(
            back.at[h, way], (from_left, from_right)[way].at[h],
            send2.at[h, way], recv2.at[h, way], (right, left)[way],
        )

    def own_copy(x, h):
        mid = pl.ds(halo, rows)
        dst = (q_own.at[h], kv.at[h, 0, mid, :], kv.at[h, 1, mid, :], g_own.at[h])[x]
        src = (q_hbm, k_hbm, v_hbm, g_hbm)[x]
        return pltpu.make_async_copy(src.at[:, pl.ds(h * d, d)], dst, own_sem.at[h, x])

    len_copy = pltpu.make_async_copy(len_hbm, len_ref, len_sem)
    len_copy.start()
    for h in range(heads):
        for x in range(4):
            own_copy(x, h).start()
    barrier = pltpu.get_barrier_semaphore()
    for who in (left, right):
        pl.semaphore_signal(barrier, inc=1, device_id=(who, ten), device_id_type=MESH)
    pl.semaphore_wait(barrier, 2)
    for way in range(2):
        for x in range(2):
            raw_copy(x, 0, way).start()

    first = me * rows
    len_copy.wait()
    begin, end = row_tables(len_ref[...], first, count)
    wide = jnp.broadcast_to(begin, (count, d))
    idc[...] = wide[halo - edge : halo + rows + edge]
    idr[...] = jnp.transpose(wide)[:8, :]
    lo = first.astype(F32)
    hi = (first + rows).astype(F32)
    b0, e0 = begin[halo : halo + 1], end[halo : halo + 1]
    spans_l = b0 < lo
    keep_l = spans_l & (e0 - lo > edge)
    moved_in_l = jnp.where(keep_l & (lo - b0 <= edge), 1.0, 0.0)
    shared_l = jnp.where(keep_l & (lo - b0 > edge), 1.0, 0.0)
    b1, e1 = begin[halo + rows - 1 : halo + rows], end[halo + rows - 1 : halo + rows]
    spans_r = e1 > hi
    moved_in_r = jnp.where(spans_r & (e1 - hi <= edge), 1.0, 0.0)
    far_r = spans_r & (e1 - hi > edge)
    moved_out_r = jnp.where(far_r & (hi - b1 <= edge), 1.0, 0.0)
    shared_r = jnp.where(far_r & (hi - b1 > edge), 1.0, 0.0)
    moved_out_l = jnp.where(spans_l & (e0 - lo <= edge), 1.0, 0.0)
    full = (edge, d)
    is_shared_l = jnp.broadcast_to(shared_l, full) > 0.5
    is_shared_r = jnp.broadcast_to(shared_r, full) > 0.5

    for h in range(heads):
        for x in range(4):
            own_copy(x, h).wait()
        if h > 0:
            for way in range(2):
                for x in range(2):
                    raw_copy(x, h, way).start()
        for x, own in ((0, q_own), (1, g_own)):
            packed[h, 0, x] = jnp.where(
                is_shared_r, kv[h, x, halo + rows - halo : halo + rows - raw, :],
                own[h, rows - edge : rows, :],
            )
            packed[h, 1, x] = jnp.where(
                is_shared_l, kv[h, x, halo + raw : halo + halo, :], own[h, 0:edge, :]
            )
        for way in range(2):
            packed_copy(h, way).start()
    for h in range(heads):
        qt[h, :, edge : edge + rows] = jnp.transpose(q_own[h])
        gt[h, :, edge : edge + rows] = jnp.transpose(g_own[h])

    factor = 1.0 / math.sqrt(d)
    last = count - edge
    half = rows // 2

    def one_head(h, carry):
        for way in range(2):
            for x in range(2):
                raw_copy(x, h, way).wait_recv()
            packed_copy(h, way).wait_recv()
        kv_q = (
            (kv[h, 0, 0:edge, :], kv[h, 1, 0:edge, :]),
            (q_own[h, 0:half, :], g_own[h, 0:half, :]),
            (q_own[h, half:rows, :], g_own[h, half:rows, :]),
            (kv[h, 0, last:count, :], kv[h, 1, last:count, :]),
        )
        qt[h, :, 0:edge] = jnp.transpose(kv_q[0][0])
        gt[h, :, 0:edge] = jnp.transpose(kv_q[0][1])
        qt[h, :, edge + rows :] = jnp.transpose(kv_q[3][0])
        gt[h, :, edge + rows :] = jnp.transpose(kv_q[3][1])
        spans = (
            (0, edge, halo - edge, halo + rows, moved_in_l),
            (edge, half, 0, count - edge, None),
            (edge + half, half, edge, count, None),
            (edge + rows, edge, halo, halo + rows + edge, moved_in_r),
        )
        outs = []
        for (qb, gb), (r0, n, k0, k1, valid) in zip(kv_q, spans):
            kb, vb = kv[h, 0, k0:k1, :], kv[h, 1, k0:k1, :]
            s = dot_nt(qb, kb) * (factor * LOG2E)
            s = jnp.where(idc[r0 : r0 + n, :1] == idr[:1, k0:k1], s, -1e30)
            top = jnp.max(s, axis=1, keepdims=True)
            w = jnp.exp2(s - top)
            total = jnp.sum(w, axis=1, keepdims=True)
            probs = w * ((1.0 if valid is None else valid) / total)
            low = probs.astype(BF)
            o = dot_nn(low, vb).astype(BF)
            p_s[r0 : r0 + n, k0:k1] = low
            gp = dot_nt(gb, vb)
            centre = jnp.sum(gb.astype(F32) * o.astype(F32), axis=1, keepdims=True)
            ds = (probs * (gp - centre)).astype(BF)
            ds_s[r0 : r0 + n, k0:k1] = ds
            dq = (dot_nn(ds, kb) * factor).astype(BF)
            outs.append((dq, o))

        def key_grads(r0, r1, c0, c1):
            dk = jnp.transpose(dot_nn(qt[h, :, r0:r1], ds_s[r0:r1, c0:c1]) * factor)
            dv = jnp.transpose(dot_nn(gt[h, :, r0:r1], p_s[r0:r1, c0:c1]))
            return dk, dv

        e, n = edge, qrows
        far = key_grads(e, e + half, 0, e)
        mid = key_grads(e, e + rows, e, 2 * e)
        near = key_grads(0, e + rows, 2 * e, 3 * e)
        for x in range(2):
            back[h, 1, x, 0:e] = jnp.where(is_shared_l, far[x].astype(BF), outs[0][x])
            back[h, 1, x, e : 2 * e] = mid[x].astype(BF)
            back[h, 1, x, 2 * e : 3 * e] = near[x].astype(BF)
        back_copy(h, 1).start()
        k = halo + rows
        near = key_grads(e, n, k, k + e)
        mid = key_grads(e, e + rows, k + e, k + 2 * e)
        far = key_grads(e + half, e + rows, k + 2 * e, k + 3 * e)
        for x in range(2):
            back[h, 0, x, 0:e] = near[x].astype(BF)
            back[h, 0, x, e : 2 * e] = mid[x].astype(BF)
            back[h, 0, x, 2 * e : 3 * e] = jnp.where(is_shared_r, far[x].astype(BF), outs[3][x])
        back_copy(h, 0).start()
        cols = pl.ds(pl.multiple_of(h * d, d), d)
        for i in range(2):
            rs = pl.ds(i * half, half)
            out_ref[1, rs, cols] = outs[1 + i][0]
            out_ref[0, rs, cols] = outs[1 + i][1]
            dk, dv = key_grads(0, n, halo + i * half, halo + (i + 1) * half)
            own_kv[h, 0, rs, :] = dk
            own_kv[h, 1, rs, :] = dv
        return carry

    lax.fori_loop(0, heads, one_head, 0)

    row_l = (begin[halo : halo + edge] < lo) & (jnp.broadcast_to(moved_out_l, (edge, 1)) > 0.5)
    row_r = (end[halo + rows - edge : halo + rows] > hi) & (
        jnp.broadcast_to(moved_out_r, (edge, 1)) > 0.5
    )
    full = (halo, d)
    add_l = jnp.broadcast_to(shared_l, full) > 0.5
    add_r = jnp.broadcast_to(shared_r, full) > 0.5
    tail = rows - edge
    for h in range(heads):
        for way in range(2):
            back_copy(h, way).wait_recv()
        cols = slice(h * d, (h + 1) * d)
        for x in range(2):
            fl = from_left[h, x].astype(F32)
            fr = from_right[h, x].astype(F32)
            out_ref[1 - x, 0:edge, cols] = jnp.where(
                row_l, from_left[h, x, 2 * edge :, :], out_ref[1 - x, 0:edge, cols]
            )
            out_ref[1 - x, tail:rows, cols] = jnp.where(
                row_r, from_right[h, x, 0:edge, :], out_ref[1 - x, tail:rows, cols]
            )
            own_kv[h, x, 0:halo, :] += jnp.where(add_l, fl, 0.0)
            own_kv[h, x, rows - halo : rows, :] += jnp.where(add_r, fr, 0.0)
            out_ref[2 + x, edge:tail, cols] = own_kv[h, x, edge:tail, :].astype(BF)
            out_ref[2 + x, 0:edge, cols] = jnp.where(
                row_l, fl[0:edge], own_kv[h, x, 0:edge, :]
            ).astype(BF)
            out_ref[2 + x, tail:rows, cols] = jnp.where(
                row_r, fr[2 * edge :], own_kv[h, x, tail:rows, :]
            ).astype(BF)
    for h in range(heads):
        for way in range(2):
            for x in range(2):
                raw_copy(x, h, way).wait_send()
            packed_copy(h, way).wait_send()
            back_copy(h, way).wait_send()


def body(queries, keys, values, out_grad, lengths):
    rows, width = queries.shape
    heads = width // D
    n_dp = lax.axis_size("dp")
    count = rows + 2 * HALO
    qrows = rows + 2 * EDGE
    pairs = qrows * count * heads
    operands = [
        pltpu.with_memory_space_constraint(x, pltpu.MemorySpace.HBM)
        for x in (queries, keys, values, out_grad, lengths.reshape(-1, 128))
    ]
    results = pl.pallas_call(
        functools.partial(kernel, n_dp, rows, heads),
        out_shape=jax.ShapeDtypeStruct((4, rows, width), BF),
        in_specs=[pl.BlockSpec(memory_space=pltpu.MemorySpace.HBM)] * 5,
        out_specs=pl.BlockSpec(memory_space=pltpu.VMEM),
        scratch_shapes=[
            pltpu.VMEM((heads, 2, count, D), BF),
            pltpu.VMEM((heads, rows, D), BF),
            pltpu.VMEM((heads, rows, D), BF),
            pltpu.VMEM((heads, D, qrows), BF),
            pltpu.VMEM((heads, D, qrows), BF),
            pltpu.VMEM((heads, 2, 2, EDGE, D), BF),
            pltpu.VMEM((heads, 2, 2, HALO, D), BF),
            pltpu.VMEM((heads, 2, HALO, D), BF),
            pltpu.VMEM((heads, 2, HALO, D), BF),
            pltpu.VMEM((qrows, D), F32),
            pltpu.VMEM((8, count), F32),
            pltpu.VMEM((qrows, count), BF),
            pltpu.VMEM((qrows, count), BF),
            pltpu.VMEM((heads, 2, rows, D), F32),
            pltpu.VMEM((lengths.shape[0] // 128, 128), jnp.int32),
            pltpu.SemaphoreType.DMA((heads, 4)),
            pltpu.SemaphoreType.DMA(()),
            pltpu.SemaphoreType.DMA((heads, 3, 2)),
            pltpu.SemaphoreType.DMA((heads, 3, 2)),
            pltpu.SemaphoreType.DMA((heads, 2)),
            pltpu.SemaphoreType.DMA((heads, 2)),
        ],
        compiler_params=pltpu.CompilerParams(
            collective_id=0, has_side_effects=True, vmem_limit_bytes=48 << 20
        ),
        cost_estimate=pl.CostEstimate(
            flops=12 * pairs * D, bytes_accessed=16 * rows * width, transcendentals=pairs
        ),
    )(*operands)
    return tuple(results[x] for x in range(4))


def solution(mesh):
    spec = P("dp", "tensor")
    return jax.shard_map(
        body, mesh=mesh, in_specs=(spec,) * 4 + (P(),), out_specs=(spec,) * 4, check_vma=False
    )
```

```python
import functools
import math

import jax
import jax.numpy as jnp
from jax import lax
from jax.experimental import pallas as pl
from jax.experimental.pallas import tpu as pltpu
from jax.sharding import PartitionSpec as P

D = 128
EDGE = 128
HALO = 384
QBLK = 256
MESH = pl.DeviceIdType.MESH
LOG2E = 1.4426950408889634
BF = jnp.bfloat16
F32 = jnp.float32


def dot_nt(a, b):
    return lax.dot_general(a, b, (((1,), (1,)), ((), ())), preferred_element_type=F32)


def dot_nn(a, b):
    return jnp.dot(a, b, preferred_element_type=F32)


def row_tables(lens, first, count):
    upper = (
        lax.broadcasted_iota(jnp.int32, (128, 128), 0)
        <= lax.broadcasted_iota(jnp.int32, (128, 128), 1)
    ).astype(F32).astype(BF)
    high = (lens >> 4).astype(F32).astype(BF)
    low = (lens & 15).astype(F32).astype(BF)
    within = 16.0 * dot_nn(high, upper) + dot_nn(low, upper)
    pos = (first - HALO + lax.broadcasted_iota(jnp.int32, (count, 128), 0)).astype(F32)
    begin = jnp.zeros((count, 128), F32)
    end = jnp.full((count, 128), 1e9, F32)
    base = jnp.zeros((1, 1), F32)
    for g in range(lens.shape[0]):
        e = within[g : g + 1, :] + base
        base = base + within[g : g + 1, 127:128]
        past = e <= pos
        begin = jnp.maximum(begin, jnp.where(past, e, 0.0))
        end = jnp.minimum(end, jnp.where(past, 1e9, e))
    begin = jnp.max(begin, axis=1, keepdims=True)
    end = jnp.min(end, axis=1, keepdims=True)
    return jnp.where(pos[:, :1] < 0.0, -1.0, begin), end


def kernel(
    n_dp, rows, heads,
    q_hbm, k_hbm, v_hbm, g_hbm, len_hbm,
    out_ref,
    kv, q_own, g_own, qt, gt, packed, back, from_left, from_right,
    idc, idr, p_s, ds_s, own_kv, len_ref,
    own_sem, len_sem, send1, recv1, send2, recv2, ready,
):
    halo, edge, d = HALO, EDGE, D
    count = rows + 2 * halo
    qrows = rows + 2 * edge
    me = lax.axis_index("dp")
    ten = lax.axis_index("tensor")
    right = lax.rem(me + 1, n_dp)
    left = lax.rem(me + n_dp - 1, n_dp)
    has_left, has_right = me > 0, me < n_dp - 1
    there = (has_right, has_left)
    here = (has_left, has_right)
    raw = halo - edge

    def remote(src, dst, send, recv, who):
        return pltpu.make_async_remote_copy(
            src_ref=src, dst_ref=dst, send_sem=send, recv_sem=recv,
            device_id=(who, ten), device_id_type=MESH,
        )

    def raw_copy(x, h, way):
        src = pl.ds(rows - raw, raw) if way == 0 else pl.ds(0, raw)
        dst = pl.ds(edge, raw) if way == 0 else pl.ds(halo + rows, raw)
        return remote(
            (k_hbm, v_hbm)[x].at[src, pl.ds(h * d, d)], kv.at[h, x, dst, :],
            send1.at[h, x, way], recv1.at[h, x, way], (right, left)[way],
        )

    def packed_copy(h, way):
        dst = pl.ds(0, edge) if way == 0 else pl.ds(count - edge, edge)
        return remote(
            packed.at[h, way], kv.at[h, :, dst, :],
            send1.at[h, 2, way], recv1.at[h, 2, way], (right, left)[way],
        )

    def back_copy(h, way):
        return remote(
            back.at[h, way], (from_left, from_right)[way].at[h],
            send2.at[h, way], recv2.at[h, way], (right, left)[way],
        )

    def own_copy(x, h):
        mid = pl.ds(halo, rows)
        dst = (q_own.at[h], kv.at[h, 0, mid, :], kv.at[h, 1, mid, :], g_own.at[h])[x]
        src = (q_hbm, k_hbm, v_hbm, g_hbm)[x]
        return pltpu.make_async_copy(src.at[:, pl.ds(h * d, d)], dst, own_sem.at[h, x])

    barrier = pltpu.get_barrier_semaphore()

    @pl.when(has_left)
    def _():
        pl.semaphore_signal(barrier, inc=1, device_id=(left, ten), device_id_type=MESH)

    len_copy = pltpu.make_async_copy(len_hbm, len_ref, len_sem)
    len_copy.start()
    for h in range(heads):
        for x in range(4):
            own_copy(x, h).start()
    @pl.when(has_right)
    def _():
        pl.semaphore_wait(barrier, 1)
        pl.semaphore_signal(ready, inc=1, device_id=(right, ten), device_id_type=MESH)
        for x in range(2):
            raw_copy(x, 0, 0).start()

    @pl.when(jnp.logical_not(has_left))
    def _():
        kv[:, :, 0:halo, :] = jnp.zeros((heads, 2, halo, d), BF)
        from_left[...] = jnp.zeros((heads, 2, halo, d), BF)

    @pl.when(jnp.logical_not(has_right))
    def _():
        kv[:, :, halo + rows :, :] = jnp.zeros((heads, 2, halo, d), BF)
        from_right[...] = jnp.zeros((heads, 2, halo, d), BF)


    first = me * rows
    len_copy.wait()
    begin, end = row_tables(len_ref[...], first, count)
    wide = jnp.broadcast_to(begin, (count, d))
    idc[...] = wide[halo - edge : halo + rows + edge]
    idr[...] = jnp.transpose(wide)[:8, :]
    lo = first.astype(F32)
    hi = (first + rows).astype(F32)
    b0, e0 = begin[halo : halo + 1], end[halo : halo + 1]
    spans_l = b0 < lo
    keep_l = spans_l & (e0 - lo > edge)
    moved_in_l = jnp.where(keep_l & (lo - b0 <= edge), 1.0, 0.0)
    shared_l = jnp.where(keep_l & (lo - b0 > edge), 1.0, 0.0)
    b1, e1 = begin[halo + rows - 1 : halo + rows], end[halo + rows - 1 : halo + rows]
    spans_r = e1 > hi
    moved_in_r = jnp.where(spans_r & (e1 - hi <= edge), 1.0, 0.0)
    far_r = spans_r & (e1 - hi > edge)
    moved_out_r = jnp.where(far_r & (hi - b1 <= edge), 1.0, 0.0)
    shared_r = jnp.where(far_r & (hi - b1 > edge), 1.0, 0.0)
    moved_out_l = jnp.where(spans_l & (e0 - lo <= edge), 1.0, 0.0)
    full = (edge, d)
    is_shared_l = jnp.broadcast_to(shared_l, full) > 0.5
    is_shared_r = jnp.broadcast_to(shared_r, full) > 0.5

    for h in range(heads):
        for x in range(4):
            own_copy(x, h).wait()
        for x, own in ((0, q_own), (1, g_own)):
            packed[h, 0, x] = jnp.where(
                is_shared_r, kv[h, x, halo + rows - halo : halo + rows - raw, :],
                own[h, rows - edge : rows, :],
            )
            packed[h, 1, x] = jnp.where(
                is_shared_l, kv[h, x, halo + raw : halo + halo, :], own[h, 0:edge, :]
            )

        @pl.when(has_right)
        def _(h=h):
            packed_copy(h, 0).start()
            if h + 1 < heads:
                for x in range(2):
                    raw_copy(x, h + 1, 0).start()

    @pl.when(has_left)
    def _():
        pl.semaphore_wait(ready, 1)
        for h in range(heads):
            for x in range(2):
                raw_copy(x, h, 1).start()
            packed_copy(h, 1).start()

    for h in range(heads):
        qt[h, :, edge : edge + rows] = jnp.transpose(q_own[h])
        gt[h, :, edge : edge + rows] = jnp.transpose(g_own[h])

    factor = 1.0 / math.sqrt(d)
    last = count - edge
    half = rows // 2

    def key_grads(h, r0, r1, c0, c1):
        dk = jnp.transpose(dot_nn(qt[h, :, r0:r1], ds_s[h, r0:r1, c0:c1]) * factor)
        dv = jnp.transpose(dot_nn(gt[h, :, r0:r1], p_s[h, r0:r1, c0:c1]))
        return dk, dv

    def one_head(h, carry):
        for way in range(2):

            @pl.when(here[way])
            def _(way=way):
                for x in range(2):
                    raw_copy(x, h, way).wait_recv()
                packed_copy(h, way).wait_recv()

        low_q, low_g = kv[h, 0, 0:edge, :], kv[h, 1, 0:edge, :]
        high_q, high_g = kv[h, 0, last:count, :], kv[h, 1, last:count, :]
        qt[h, :, 0:edge] = jnp.transpose(low_q)
        gt[h, :, 0:edge] = jnp.transpose(low_g)
        qt[h, :, edge + rows :] = jnp.transpose(high_q)
        gt[h, :, edge + rows :] = jnp.transpose(high_g)
        blocks = [(low_q, low_g, 0, edge, halo - edge, halo + rows, moved_in_l)]
        for r0 in range(0, rows, QBLK):
            k0 = max(0, (r0 + 1 - rows + halo) // 128 * 128)
            k1 = min(count, -(-(r0 + QBLK - 1 + rows + halo) // 128) * 128)
            rs = slice(r0, r0 + QBLK)
            blocks.append((q_own[h, rs, :], g_own[h, rs, :], edge + r0, QBLK, k0, k1, None))
        blocks.append((high_q, high_g, edge + rows, edge, halo, halo + rows + edge, moved_in_r))
        outs = []
        for qb, gb, r0, n, k0, k1, valid in blocks:
            kb, vb = kv[h, 0, k0:k1, :], kv[h, 1, k0:k1, :]
            s = dot_nt(qb, kb) * (factor * LOG2E)
            s = jnp.where(idc[r0 : r0 + n, :1] == idr[:1, k0:k1], s, -1e30)
            top = jnp.max(s, axis=1, keepdims=True)
            w = jnp.exp2(s - top)
            total = jnp.sum(w, axis=1, keepdims=True)
            probs = w * ((1.0 if valid is None else valid) / total)
            low = probs.astype(BF)
            o = dot_nn(low, vb).astype(BF)
            p_s[h, r0 : r0 + n, k0:k1] = low
            gp = dot_nt(gb, vb)
            centre = jnp.sum(gb.astype(F32) * o.astype(F32), axis=1, keepdims=True)
            ds = (probs * (gp - centre)).astype(BF)
            ds_s[h, r0 : r0 + n, k0:k1] = ds
            dq = (dot_nn(ds, kb) * factor).astype(BF)
            outs.append((dq, o))

        e, n, k = edge, qrows, halo + rows
        near = key_grads(h, e, n, k, k + e)
        mid = key_grads(h, e, e + rows, k + e, k + 2 * e)
        far = key_grads(h, e + half, e + rows, k + 2 * e, k + 3 * e)
        for x in range(2):
            back[h, 0, x, 0:e] = near[x].astype(BF)
            back[h, 0, x, e : 2 * e] = mid[x].astype(BF)
            back[h, 0, x, 2 * e : 3 * e] = jnp.where(is_shared_r, far[x].astype(BF), outs[-1][x])

        @pl.when(there[0])
        def _():
            back_copy(h, 0).start()

        far = key_grads(h, e, e + half, 0, e)
        mid = key_grads(h, e, e + rows, e, 2 * e)
        near = key_grads(h, 0, e + rows, 2 * e, 3 * e)
        for x in range(2):
            back[h, 1, x, 0:e] = jnp.where(is_shared_l, far[x].astype(BF), outs[0][x])
            back[h, 1, x, e : 2 * e] = mid[x].astype(BF)
            back[h, 1, x, 2 * e : 3 * e] = near[x].astype(BF)

        @pl.when(there[1])
        def _():
            back_copy(h, 1).start()

        cols = pl.ds(pl.multiple_of(h * d, d), d)
        for i in range(rows // QBLK):
            rs = pl.ds(i * QBLK, QBLK)
            out_ref[1, rs, cols] = outs[1 + i][0]
            out_ref[0, rs, cols] = outs[1 + i][1]
        return carry

    lax.fori_loop(0, heads, one_head, 0)

    def own_key_grads(h, carry):
        for i in range(2):
            rs = pl.ds(i * half, half)
            dk, dv = key_grads(h, 0, qrows, halo + i * half, halo + (i + 1) * half)
            own_kv[h, 0, rs, :] = dk
            own_kv[h, 1, rs, :] = dv
        return carry

    lax.fori_loop(0, heads, own_key_grads, 0)

    row_l = (begin[halo : halo + edge] < lo) & (jnp.broadcast_to(moved_out_l, (edge, 1)) > 0.5)
    row_r = (end[halo + rows - edge : halo + rows] > hi) & (
        jnp.broadcast_to(moved_out_r, (edge, 1)) > 0.5
    )
    full = (halo, d)
    add_l = jnp.broadcast_to(shared_l, full) > 0.5
    add_r = jnp.broadcast_to(shared_r, full) > 0.5
    tail = rows - edge
    for h in range(heads):
        for way in range(2):

            @pl.when(here[way])
            def _(h=h, way=way):
                back_copy(h, way).wait_recv()

        cols = slice(h * d, (h + 1) * d)
        for x in range(2):
            fl = from_left[h, x].astype(F32)
            fr = from_right[h, x].astype(F32)
            out_ref[1 - x, 0:edge, cols] = jnp.where(
                row_l, from_left[h, x, 2 * edge :, :], out_ref[1 - x, 0:edge, cols]
            )
            out_ref[1 - x, tail:rows, cols] = jnp.where(
                row_r, from_right[h, x, 0:edge, :], out_ref[1 - x, tail:rows, cols]
            )
            own_kv[h, x, 0:halo, :] += jnp.where(add_l, fl, 0.0)
            own_kv[h, x, rows - halo : rows, :] += jnp.where(add_r, fr, 0.0)
            out_ref[2 + x, edge:tail, cols] = own_kv[h, x, edge:tail, :].astype(BF)
            out_ref[2 + x, 0:edge, cols] = jnp.where(
                row_l, fl[0:edge], own_kv[h, x, 0:edge, :]
            ).astype(BF)
            out_ref[2 + x, tail:rows, cols] = jnp.where(
                row_r, fr[2 * edge :], own_kv[h, x, tail:rows, :]
            ).astype(BF)
    for h in range(heads):
        for way in range(2):

            @pl.when(there[way])
            def _(h=h, way=way):
                for x in range(2):
                    raw_copy(x, h, way).wait_send()
                packed_copy(h, way).wait_send()
                back_copy(h, way).wait_send()


def body(queries, keys, values, out_grad, lengths):
    rows, width = queries.shape
    heads = width // D
    n_dp = lax.axis_size("dp")
    count = rows + 2 * HALO
    qrows = rows + 2 * EDGE
    pairs = qrows * count * heads
    operands = [
        pltpu.with_memory_space_constraint(x, pltpu.MemorySpace.HBM)
        for x in (queries, keys, values, out_grad, lengths.reshape(-1, 128))
    ]
    results = pl.pallas_call(
        functools.partial(kernel, n_dp, rows, heads),
        out_shape=jax.ShapeDtypeStruct((4, rows, width), BF),
        in_specs=[pl.BlockSpec(memory_space=pltpu.MemorySpace.HBM)] * 5,
        out_specs=pl.BlockSpec(memory_space=pltpu.VMEM),
        scratch_shapes=[
            pltpu.VMEM((heads, 2, count, D), BF),
            pltpu.VMEM((heads, rows, D), BF),
            pltpu.VMEM((heads, rows, D), BF),
            pltpu.VMEM((heads, D, qrows), BF),
            pltpu.VMEM((heads, D, qrows), BF),
            pltpu.VMEM((heads, 2, 2, EDGE, D), BF),
            pltpu.VMEM((heads, 2, 2, HALO, D), BF),
            pltpu.VMEM((heads, 2, HALO, D), BF),
            pltpu.VMEM((heads, 2, HALO, D), BF),
            pltpu.VMEM((qrows, D), F32),
            pltpu.VMEM((8, count), F32),
            pltpu.VMEM((heads, qrows, count), BF),
            pltpu.VMEM((heads, qrows, count), BF),
            pltpu.VMEM((heads, 2, rows, D), F32),
            pltpu.VMEM((lengths.shape[0] // 128, 128), jnp.int32),
            pltpu.SemaphoreType.DMA((heads, 4)),
            pltpu.SemaphoreType.DMA(()),
            pltpu.SemaphoreType.DMA((heads, 3, 2)),
            pltpu.SemaphoreType.DMA((heads, 3, 2)),
            pltpu.SemaphoreType.DMA((heads, 2)),
            pltpu.SemaphoreType.DMA((heads, 2)),
            pltpu.SemaphoreType.REGULAR,
        ],
        compiler_params=pltpu.CompilerParams(
            collective_id=0, has_side_effects=True, vmem_limit_bytes=48 << 20
        ),
        cost_estimate=pl.CostEstimate(
            flops=12 * pairs * D, bytes_accessed=16 * rows * width, transcendentals=pairs
        ),
    )(*operands)
    return tuple(results[x] for x in range(4))


def solution(mesh):
    spec = P("dp", "tensor")
    return jax.shard_map(
        body, mesh=mesh, in_specs=(spec,) * 4 + (P(),), out_specs=(spec,) * 4, check_vma=False
    )
```

```python
import functools
import math

import jax
import jax.numpy as jnp
from jax import lax
from jax.experimental import pallas as pl
from jax.experimental.pallas import tpu as pltpu
from jax.sharding import PartitionSpec as P

D = 128
EDGE_L, EDGE_R = 192, 128
HALO_L, HALO_R = 384, 320
PAD = 64
MESH = pl.DeviceIdType.MESH
LOG2E = 1.4426950408889634
BF = jnp.bfloat16
F32 = jnp.float32


def dot_nt(a, b):
    return lax.dot_general(a, b, (((1,), (1,)), ((), ())), preferred_element_type=F32)


def dot_nn(a, b):
    return jnp.dot(a, b, preferred_element_type=F32)


def row_tables(lens, first, count):
    upper = (
        lax.broadcasted_iota(jnp.int32, (128, 128), 0)
        <= lax.broadcasted_iota(jnp.int32, (128, 128), 1)
    ).astype(F32).astype(BF)
    high = (lens >> 4).astype(F32).astype(BF)
    low = (lens & 15).astype(F32).astype(BF)
    within = 16.0 * dot_nn(high, upper) + dot_nn(low, upper)
    pos = (first - HALO_L + lax.broadcasted_iota(jnp.int32, (count, 128), 0)).astype(F32)
    begin = jnp.zeros((count, 128), F32)
    end = jnp.full((count, 128), 1e9, F32)
    base = jnp.zeros((1, 1), F32)
    for g in range(lens.shape[0]):
        e = within[g : g + 1, :] + base
        base = base + within[g : g + 1, 127:128]
        past = e <= pos
        begin = jnp.maximum(begin, jnp.where(past, e, 0.0))
        end = jnp.minimum(end, jnp.where(past, 1e9, e))
    begin = jnp.max(begin, axis=1, keepdims=True)
    end = jnp.min(end, axis=1, keepdims=True)
    return jnp.where(pos[:, :1] < 0.0, -1.0, begin), end


def kernel(
    n_dp, rows, heads,
    q_hbm, k_hbm, v_hbm, g_hbm, len_hbm,
    out_ref,
    kv, q_own, g_own, qt, gt, packed_r, packed_l, back_r, back_l, from_left, from_right,
    idc, idr, p_s, ds_s, own_kv, len_ref,
    own_sem, len_sem, send1, recv1, send2, recv2, ready,
):
    hl, hr, el, er, d = HALO_L, HALO_R, EDGE_L, EDGE_R, D
    count = hl + rows + hr + PAD
    qrows = el + rows + er
    me = lax.axis_index("dp")
    ten = lax.axis_index("tensor")
    right = lax.rem(me + 1, n_dp)
    left = lax.rem(me + n_dp - 1, n_dp)
    has_left, has_right = me > 0, me < n_dp - 1
    there = (has_right, has_left)
    here = (has_left, has_right)
    raw = hl - el
    assert raw == hr - er

    def remote(src, dst, send, recv, who):
        return pltpu.make_async_remote_copy(
            src_ref=src, dst_ref=dst, send_sem=send, recv_sem=recv,
            device_id=(who, ten), device_id_type=MESH,
        )

    def raw_copy(x, h, way):
        src = pl.ds(rows - raw, raw) if way == 0 else pl.ds(0, raw)
        dst = pl.ds(el, raw) if way == 0 else pl.ds(hl + rows, raw)
        return remote(
            (k_hbm, v_hbm)[x].at[src, pl.ds(h * d, d)], kv.at[h, x, dst, :],
            send1.at[h, x, way], recv1.at[h, x, way], (right, left)[way],
        )

    def packed_copy(h, way):
        dst = pl.ds(0, el) if way == 0 else pl.ds(hl + rows + raw, er)
        return remote(
            (packed_r, packed_l)[way].at[h], kv.at[h, :, dst, :],
            send1.at[h, 2, way], recv1.at[h, 2, way], (right, left)[way],
        )

    def back_copy(h, way):
        return remote(
            (back_r, back_l)[way].at[h], (from_left, from_right)[way].at[h],
            send2.at[h, way], recv2.at[h, way], (right, left)[way],
        )

    def own_copy(x, h):
        mid = pl.ds(hl, rows)
        dst = (q_own.at[h], kv.at[h, 0, mid, :], kv.at[h, 1, mid, :], g_own.at[h])[x]
        src = (q_hbm, k_hbm, v_hbm, g_hbm)[x]
        return pltpu.make_async_copy(src.at[:, pl.ds(h * d, d)], dst, own_sem.at[h, x])

    barrier = pltpu.get_barrier_semaphore()

    @pl.when(has_left)
    def _():
        pl.semaphore_signal(barrier, inc=1, device_id=(left, ten), device_id_type=MESH)

    len_copy = pltpu.make_async_copy(len_hbm, len_ref, len_sem)
    len_copy.start()
    for h in range(heads):
        for x in range(4):
            own_copy(x, h).start()
    @pl.when(has_right)
    def _():
        pl.semaphore_wait(barrier, 1)
        pl.semaphore_signal(ready, inc=1, device_id=(right, ten), device_id_type=MESH)
        for x in range(2):
            raw_copy(x, 0, 0).start()

    @pl.when(jnp.logical_not(has_left))
    def _():
        kv[:, :, 0:hl, :] = jnp.zeros((heads, 2, hl, d), BF)
        from_left[...] = jnp.zeros((heads, 2, hr, d), BF)

    @pl.when(jnp.logical_not(has_right))
    def _():
        kv[:, :, hl + rows : hl + rows + hr, :] = jnp.zeros((heads, 2, hr, d), BF)
        from_right[...] = jnp.zeros((heads, 2, hl, d), BF)


    kv[:, :, count - PAD :, :] = jnp.zeros((heads, 2, PAD, d), BF)
    first = me * rows
    len_copy.wait()
    begin, end = row_tables(len_ref[...], first, count)
    wide = jnp.broadcast_to(begin, (count, d))
    idc[...] = wide[hl - el : hl + rows + er]
    idr[...] = jnp.transpose(wide)[:8, :]
    lo = first.astype(F32)
    hi = (first + rows).astype(F32)
    b0, e0 = begin[hl : hl + 1], end[hl : hl + 1]
    spans_l = b0 < lo
    keep_l = spans_l & (e0 - lo > er)
    moved_in_l = jnp.where(keep_l & (lo - b0 <= el), 1.0, 0.0)
    shared_l = jnp.where(keep_l & (lo - b0 > el), 1.0, 0.0)
    b1, e1 = begin[hl + rows - 1 : hl + rows], end[hl + rows - 1 : hl + rows]
    spans_r = e1 > hi
    moved_in_r = jnp.where(spans_r & (e1 - hi <= er), 1.0, 0.0)
    far_r = spans_r & (e1 - hi > er)
    moved_out_r = jnp.where(far_r & (hi - b1 <= el), 1.0, 0.0)
    shared_r = jnp.where(far_r & (hi - b1 > el), 1.0, 0.0)
    moved_out_l = jnp.where(spans_l & (e0 - lo <= er), 1.0, 0.0)

    def mask(flag, n):
        return jnp.broadcast_to(flag, (n, d)) > 0.5


    for h in range(heads):
        for x in range(4):
            own_copy(x, h).wait()
        for x, own in ((0, q_own), (1, g_own)):
            packed_r[h, x] = jnp.where(
                mask(shared_r, el), kv[h, x, rows : rows + el, :], own[h, rows - el : rows, :]
            )
            packed_l[h, x] = jnp.where(
                mask(shared_l, er), kv[h, x, hl + raw : hl + raw + er, :], own[h, 0:er, :]
            )

        @pl.when(has_right)
        def _(h=h):
            packed_copy(h, 0).start()
            if h + 1 < heads:
                for x in range(2):
                    raw_copy(x, h + 1, 0).start()

    @pl.when(has_left)
    def _():
        pl.semaphore_wait(ready, 1)
        for h in range(heads):
            for x in range(2):
                raw_copy(x, h, 1).start()
            packed_copy(h, 1).start()

    for h in range(heads):
        qt[h, :, 0:rows] = jnp.transpose(q_own[h])
        gt[h, :, 0:rows] = jnp.transpose(g_own[h])

    factor = 1.0 / math.sqrt(d)
    half = rows // 2
    k = hl + rows
    low, high = slice(0, el), slice(k + raw, k + raw + er)

    def query_block(h, qb, gb, r0, n, k0, k1, valid):
        kb, vb = kv[h, 0, k0:k1, :], kv[h, 1, k0:k1, :]
        s = dot_nt(qb, kb) * (factor * LOG2E)
        s = jnp.where(idc[r0 : r0 + n, :1] == idr[:1, k0:k1], s, -1e30)
        top = jnp.max(s, axis=1, keepdims=True)
        w = jnp.exp2(s - top)
        total = jnp.sum(w, axis=1, keepdims=True)
        probs = w * ((1.0 if valid is None else valid) / total)
        p = probs.astype(BF)
        o = dot_nn(p, vb).astype(BF)
        p_s[h, r0 : r0 + n, k0:k1] = p
        gp = dot_nt(gb, vb)
        centre = jnp.sum(gb.astype(F32) * o.astype(F32), axis=1, keepdims=True)
        ds = (probs * (gp - centre)).astype(BF)
        ds_s[h, r0 : r0 + n, k0:k1] = ds
        return (dot_nn(ds, kb) * factor).astype(BF), o

    def key_grads(h, c0, c1, own=(0, rows), from_low=False, from_high=False):
        cs = slice(c0, c1)
        rs = slice(el + own[0], el + own[1])
        dk = dot_nn(qt[h, :, own[0] : own[1]], ds_s[h, rs, cs])
        dv = dot_nn(gt[h, :, own[0] : own[1]], p_s[h, rs, cs])
        if from_high:
            rs = slice(el + rows, qrows)
            dk += dot_nn(qt[h, :, rows : rows + er], ds_s[h, rs, cs])
            dv += dot_nn(gt[h, :, rows : rows + er], p_s[h, rs, cs])
        if from_low:
            rs, ts = slice(0, el), slice(rows + er, rows + er + el)
            dk += dot_nn(qt[h, :, ts], ds_s[h, rs, cs])
            dv += dot_nn(gt[h, :, ts], p_s[h, rs, cs])
        return jnp.transpose(dk * factor), jnp.transpose(dv)

    def right_side(h, carry):
        for way in range(2):

            @pl.when(here[way])
            def _(way=way):
                for x in range(2):
                    raw_copy(x, h, way).wait_recv()
                packed_copy(h, way).wait_recv()

        cols = pl.ds(pl.multiple_of(h * d, d), d)
        for r0 in range(0, rows, half):
            k0 = max(0, (r0 + 1 - rows + hl) // 128 * 128)
            k1 = min(count, -(-(r0 + half - 1 + rows + hl) // 128) * 128)
            rs = slice(r0, r0 + half)
            dq, o = query_block(h, q_own[h, rs, :], g_own[h, rs, :], el + r0, half, k0, k1, None)
            out_ref[1, rs, cols] = dq
            out_ref[0, rs, cols] = o
        qb, gb = kv[h, 0, high, :], kv[h, 1, high, :]
        qt[h, :, rows : rows + er] = jnp.transpose(qb)
        gt[h, :, rows : rows + er] = jnp.transpose(gb)
        moved = query_block(h, qb, gb, el + rows, er, hl, k + er, moved_in_r)
        near = key_grads(h, k, k + 128, from_high=True)
        mid = key_grads(h, k + 128, k + 256)
        far = key_grads(h, k + 256, k + 384, own=(half, rows))
        for x in range(2):
            back_r[h, x, 0:128] = near[x].astype(BF)
            back_r[h, x, 128:raw] = mid[x][0 : raw - 128].astype(BF)
            tail = jnp.concatenate([mid[x][raw - 128 :], far[x][0 : hr - 256]], axis=0)
            back_r[h, x, raw:hr] = jnp.where(mask(shared_r, er), tail.astype(BF), moved[x])

        @pl.when(has_right)
        def _():
            back_copy(h, 0).start()

        return carry


    def left_side(h, carry):
        qb, gb = kv[h, 0, low, :], kv[h, 1, low, :]
        qt[h, :, rows + er : rows + er + el] = jnp.transpose(qb)
        gt[h, :, rows + er : rows + er + el] = jnp.transpose(gb)
        moved = query_block(h, qb, gb, 0, el, hl - 256, k, moved_in_l)
        far = key_grads(h, 0, 128, own=(0, half))
        mid = key_grads(h, 128, 256, from_low=True)
        near = key_grads(h, 256, 384, from_low=True)
        for x in range(2):
            head = jnp.concatenate([far[x], mid[x][0 : el - 128]], axis=0)
            back_l[h, x, 0:el] = jnp.where(mask(shared_l, el), head.astype(BF), moved[x])
            back_l[h, x, el:256] = mid[x][el - 128 :].astype(BF)
            back_l[h, x, 256:hl] = near[x].astype(BF)

        @pl.when(has_left)
        def _():
            back_copy(h, 1).start()

        return carry

    lax.fori_loop(0, heads, lambda h, c: left_side(h, right_side(h, c)), 0)

    def own_key_grads(h, carry):
        for i in range(2):
            rs = pl.ds(i * half, half)
            own_kv[h, 0, rs, :], own_kv[h, 1, rs, :] = key_grads(
                h, hl + i * half, hl + (i + 1) * half, from_low=True, from_high=True
            )
        return carry

    lax.fori_loop(0, heads, own_key_grads, 0)

    row_l = (begin[hl : hl + er] < lo) & (jnp.broadcast_to(moved_out_l, (er, 1)) > 0.5)
    row_r = (end[k - el : k] > hi) & (jnp.broadcast_to(moved_out_r, (el, 1)) > 0.5)
    add_l, add_r = mask(shared_l, hr), mask(shared_r, hl)
    tail = rows - el
    for h in range(heads):
        for way in range(2):

            @pl.when(here[way])
            def _(h=h, way=way):
                back_copy(h, way).wait_recv()

        cols = slice(h * d, (h + 1) * d)
        for x in range(2):
            fl = from_left[h, x].astype(F32)
            fr = from_right[h, x].astype(F32)
            out_ref[1 - x, 0:er, cols] = jnp.where(
                row_l, from_left[h, x, raw:hr, :], out_ref[1 - x, 0:er, cols]
            )
            out_ref[1 - x, tail:rows, cols] = jnp.where(
                row_r, from_right[h, x, 0:el, :], out_ref[1 - x, tail:rows, cols]
            )
            own_kv[h, x, 0:hr, :] += jnp.where(add_l, fl, 0.0)
            own_kv[h, x, rows - hl : rows, :] += jnp.where(add_r, fr, 0.0)
            out_ref[2 + x, er:tail, cols] = own_kv[h, x, er:tail, :].astype(BF)
            out_ref[2 + x, 0:er, cols] = jnp.where(
                row_l, fl[0:er], own_kv[h, x, 0:er, :]
            ).astype(BF)
            out_ref[2 + x, tail:rows, cols] = jnp.where(
                row_r, fr[hl - el :], own_kv[h, x, tail:rows, :]
            ).astype(BF)
    for h in range(heads):
        for way in range(2):

            @pl.when(there[way])
            def _(h=h, way=way):
                for x in range(2):
                    raw_copy(x, h, way).wait_send()
                packed_copy(h, way).wait_send()
                back_copy(h, way).wait_send()


def body(queries, keys, values, out_grad, lengths):
    rows, width = queries.shape
    heads = width // D
    n_dp = lax.axis_size("dp")
    count = HALO_L + rows + HALO_R + PAD
    qrows = EDGE_L + rows + EDGE_R
    pairs = qrows * count * heads
    operands = [
        pltpu.with_memory_space_constraint(x, pltpu.MemorySpace.HBM)
        for x in (queries, keys, values, out_grad, lengths.reshape(-1, 128))
    ]
    results = pl.pallas_call(
        functools.partial(kernel, n_dp, rows, heads),
        out_shape=jax.ShapeDtypeStruct((4, rows, width), BF),
        in_specs=[pl.BlockSpec(memory_space=pltpu.MemorySpace.HBM)] * 5,
        out_specs=pl.BlockSpec(memory_space=pltpu.VMEM),
        scratch_shapes=[
            pltpu.VMEM((heads, 2, count, D), BF),
            pltpu.VMEM((heads, rows, D), BF),
            pltpu.VMEM((heads, rows, D), BF),
            pltpu.VMEM((heads, D, qrows), BF),
            pltpu.VMEM((heads, D, qrows), BF),
            pltpu.VMEM((heads, 2, EDGE_L, D), BF),
            pltpu.VMEM((heads, 2, EDGE_R, D), BF),
            pltpu.VMEM((heads, 2, HALO_R, D), BF),
            pltpu.VMEM((heads, 2, HALO_L, D), BF),
            pltpu.VMEM((heads, 2, HALO_R, D), BF),
            pltpu.VMEM((heads, 2, HALO_L, D), BF),
            pltpu.VMEM((qrows, D), F32),
            pltpu.VMEM((8, count), F32),
            pltpu.VMEM((heads, qrows, count), BF),
            pltpu.VMEM((heads, qrows, count), BF),
            pltpu.VMEM((heads, 2, rows, D), F32),
            pltpu.VMEM((lengths.shape[0] // 128, 128), jnp.int32),
            pltpu.SemaphoreType.DMA((heads, 4)),
            pltpu.SemaphoreType.DMA(()),
            pltpu.SemaphoreType.DMA((heads, 3, 2)),
            pltpu.SemaphoreType.DMA((heads, 3, 2)),
            pltpu.SemaphoreType.DMA((heads, 2)),
            pltpu.SemaphoreType.DMA((heads, 2)),
            pltpu.SemaphoreType.REGULAR,
        ],
        compiler_params=pltpu.CompilerParams(
            collective_id=0, has_side_effects=True, vmem_limit_bytes=48 << 20
        ),
        cost_estimate=pl.CostEstimate(
            flops=12 * pairs * D, bytes_accessed=16 * rows * width, transcendentals=pairs
        ),
    )(*operands)
    return tuple(results[x] for x in range(4))


def solution(mesh):
    spec = P("dp", "tensor")
    return jax.shard_map(
        body, mesh=mesh, in_specs=(spec,) * 4 + (P(),), out_specs=(spec,) * 4, check_vma=False
    )
```

```python
import functools
import math

import jax
import jax.numpy as jnp
from jax import lax
from jax.experimental import pallas as pl
from jax.experimental.pallas import tpu as pltpu
from jax.sharding import PartitionSpec as P

D = 128
EDGE_L, EDGE_R = 192, 128
HALO_L, HALO_R = 384, 320
PAD = 64
MESH = pl.DeviceIdType.MESH
LOG2E = 1.4426950408889634
BF = jnp.bfloat16
F32 = jnp.float32


def dot_nt(a, b):
    return lax.dot_general(a, b, (((1,), (1,)), ((), ())), preferred_element_type=F32)


def dot_nn(a, b):
    return jnp.dot(a, b, preferred_element_type=F32)


def row_tables(lens, first, count):
    upper = (
        lax.broadcasted_iota(jnp.int32, (128, 128), 0)
        <= lax.broadcasted_iota(jnp.int32, (128, 128), 1)
    ).astype(F32).astype(BF)
    high = (lens >> 4).astype(F32).astype(BF)
    low = (lens & 15).astype(F32).astype(BF)
    within = 16.0 * dot_nn(high, upper) + dot_nn(low, upper)
    pos = (first - HALO_L + lax.broadcasted_iota(jnp.int32, (count, 128), 0)).astype(F32)
    begin = jnp.zeros((count, 128), F32)
    end = jnp.full((count, 128), 1e9, F32)
    base = jnp.zeros((1, 1), F32)
    for g in range(lens.shape[0]):
        e = within[g : g + 1, :] + base
        base = base + within[g : g + 1, 127:128]
        past = e <= pos
        begin = jnp.maximum(begin, jnp.where(past, e, 0.0))
        end = jnp.minimum(end, jnp.where(past, 1e9, e))
    begin = jnp.max(begin, axis=1, keepdims=True)
    end = jnp.min(end, axis=1, keepdims=True)
    return jnp.where(pos[:, :1] < 0.0, -1.0, begin), end


def kernel(
    n_dp, rows, heads,
    q_hbm, k_hbm, v_hbm, g_hbm, len_hbm,
    out_ref,
    kv, q_own, g_own, qt, gt, packed_r, packed_l, back_r, back_l, from_left, from_right,
    idc, idr, p_s, ds_s, own_kv, len_ref,
    own_sem, len_sem, send1, recv1, send2, recv2, ready,
):
    hl, hr, el, er, d = HALO_L, HALO_R, EDGE_L, EDGE_R, D
    count = hl + rows + hr + PAD
    qrows = el + rows + er
    me = lax.axis_index("dp")
    ten = lax.axis_index("tensor")
    right = lax.rem(me + 1, n_dp)
    left = lax.rem(me + n_dp - 1, n_dp)
    has_left, has_right = me > 0, me < n_dp - 1
    there = (has_right, has_left)
    here = (has_left, has_right)
    raw = hl - el
    assert raw == hr - er

    def remote(src, dst, send, recv, who):
        return pltpu.make_async_remote_copy(
            src_ref=src, dst_ref=dst, send_sem=send, recv_sem=recv,
            device_id=(who, ten), device_id_type=MESH,
        )

    def raw_copy(x, h, way):
        src = pl.ds(rows - raw, raw) if way == 0 else pl.ds(0, raw)
        dst = pl.ds(el, raw) if way == 0 else pl.ds(hl + rows, raw)
        return remote(
            (k_hbm, v_hbm)[x].at[src, pl.ds(h * d, d)], kv.at[h, x, dst, :],
            send1.at[h, x, way], recv1.at[h, x, way], (right, left)[way],
        )

    def packed_copy(h, way):
        dst = pl.ds(0, el) if way == 0 else pl.ds(hl + rows + raw, er)
        return remote(
            (packed_r, packed_l)[way].at[h], kv.at[h, :, dst, :],
            send1.at[h, 2, way], recv1.at[h, 2, way], (right, left)[way],
        )

    def back_copy(h, way):
        return remote(
            (back_r, back_l)[way].at[h], (from_left, from_right)[way].at[h],
            send2.at[h, way], recv2.at[h, way], (right, left)[way],
        )

    def own_copy(x, h):
        mid = pl.ds(hl, rows)
        dst = (q_own.at[h], kv.at[h, 0, mid, :], kv.at[h, 1, mid, :], g_own.at[h])[x]
        src = (q_hbm, k_hbm, v_hbm, g_hbm)[x]
        return pltpu.make_async_copy(src.at[:, pl.ds(h * d, d)], dst, own_sem.at[h, x])

    barrier = pltpu.get_barrier_semaphore()

    @pl.when(has_left)
    def _():
        pl.semaphore_signal(barrier, inc=1, device_id=(left, ten), device_id_type=MESH)

    len_copy = pltpu.make_async_copy(len_hbm, len_ref, len_sem)
    len_copy.start()
    for h in range(heads):
        for x in range(4):
            own_copy(x, h).start()
    @pl.when(has_right)
    def _():
        pl.semaphore_wait(barrier, 1)
        pl.semaphore_signal(ready, inc=1, device_id=(right, ten), device_id_type=MESH)
        for x in range(2):
            raw_copy(x, 0, 0).start()

    @pl.when(jnp.logical_not(has_left))
    def _():
        kv[:, :, 0:hl, :] = jnp.zeros((heads, 2, hl, d), BF)
        from_left[...] = jnp.zeros((heads, 2, hr, d), BF)

    @pl.when(jnp.logical_not(has_right))
    def _():
        kv[:, :, hl + rows : hl + rows + hr, :] = jnp.zeros((heads, 2, hr, d), BF)
        from_right[...] = jnp.zeros((heads, 2, hl, d), BF)


    kv[:, :, count - PAD :, :] = jnp.zeros((heads, 2, PAD, d), BF)
    first = me * rows
    len_copy.wait()
    begin, end = row_tables(len_ref[...], first, count)
    wide = jnp.broadcast_to(begin, (count, d))
    idc[...] = wide[hl - el : hl + rows + er]
    idr[...] = jnp.transpose(wide)[:8, :]
    lo = first.astype(F32)
    hi = (first + rows).astype(F32)
    b0, e0 = begin[hl : hl + 1], end[hl : hl + 1]
    spans_l = b0 < lo
    keep_l = spans_l & (e0 - lo > er)
    moved_in_l = jnp.where(keep_l & (lo - b0 <= el), 1.0, 0.0)
    shared_l = jnp.where(keep_l & (lo - b0 > el), 1.0, 0.0)
    b1, e1 = begin[hl + rows - 1 : hl + rows], end[hl + rows - 1 : hl + rows]
    spans_r = e1 > hi
    moved_in_r = jnp.where(spans_r & (e1 - hi <= er), 1.0, 0.0)
    far_r = spans_r & (e1 - hi > er)
    moved_out_r = jnp.where(far_r & (hi - b1 <= el), 1.0, 0.0)
    shared_r = jnp.where(far_r & (hi - b1 > el), 1.0, 0.0)
    moved_out_l = jnp.where(spans_l & (e0 - lo <= er), 1.0, 0.0)

    def mask(flag, n):
        return jnp.broadcast_to(flag, (n, d)) > 0.5


    for h in range(heads):
        for x in range(4):
            own_copy(x, h).wait()
        for x, own in ((0, q_own), (1, g_own)):
            packed_r[h, x] = jnp.where(
                mask(shared_r, el), kv[h, x, rows : rows + el, :], own[h, rows - el : rows, :]
            )
            packed_l[h, x] = jnp.where(
                mask(shared_l, er), kv[h, x, hl + raw : hl + raw + er, :], own[h, 0:er, :]
            )

        @pl.when(has_right)
        def _(h=h):
            packed_copy(h, 0).start()
            if h + 1 < heads:
                for x in range(2):
                    raw_copy(x, h + 1, 0).start()

    @pl.when(has_left)
    def _():
        pl.semaphore_wait(ready, 1)
        for h in range(heads):
            for x in range(2):
                raw_copy(x, h, 1).start()
            packed_copy(h, 1).start()

    for h in range(heads):
        qt[h, :, 0:rows] = jnp.transpose(q_own[h])
        gt[h, :, 0:rows] = jnp.transpose(g_own[h])

    factor = 1.0 / math.sqrt(d)
    half = rows // 2
    k = hl + rows
    low, high = slice(0, el), slice(k + raw, k + raw + er)

    def query_block(h, qb, gb, r0, n, k0, k1, valid):
        kb, vb = kv[h, 0, k0:k1, :], kv[h, 1, k0:k1, :]
        s = dot_nt(qb, kb) * (factor * LOG2E)
        s = jnp.where(idc[r0 : r0 + n, :1] == idr[:1, k0:k1], s, -1e30)
        top = jnp.max(s, axis=1, keepdims=True)
        w = jnp.exp2(s - top)
        total = jnp.sum(w, axis=1, keepdims=True)
        probs = w * ((1.0 if valid is None else valid) / total)
        p = probs.astype(BF)
        o = dot_nn(p, vb).astype(BF)
        p_s[h, r0 : r0 + n, k0:k1] = p
        gp = dot_nt(gb, vb)
        centre = jnp.sum(gb.astype(F32) * o.astype(F32), axis=1, keepdims=True)
        ds = (probs * (gp - centre)).astype(BF)
        ds_s[h, r0 : r0 + n, k0:k1] = ds
        return (dot_nn(ds, kb) * factor).astype(BF), o

    def key_grads(h, c0, c1, own=(0, rows), from_low=False, from_high=False):
        cs = slice(c0, c1)
        rs = slice(el + own[0], el + own[1])
        dk = dot_nn(qt[h, :, own[0] : own[1]], ds_s[h, rs, cs])
        dv = dot_nn(gt[h, :, own[0] : own[1]], p_s[h, rs, cs])
        if from_high:
            rs = slice(el + rows, qrows)
            dk += dot_nn(qt[h, :, rows : rows + er], ds_s[h, rs, cs])
            dv += dot_nn(gt[h, :, rows : rows + er], p_s[h, rs, cs])
        if from_low:
            rs, ts = slice(0, el), slice(rows + er, rows + er + el)
            dk += dot_nn(qt[h, :, ts], ds_s[h, rs, cs])
            dv += dot_nn(gt[h, :, ts], p_s[h, rs, cs])
        return jnp.transpose(dk * factor), jnp.transpose(dv)

    def right_side(h, carry):
        for way in range(2):

            @pl.when(here[way])
            def _(way=way):
                for x in range(2):
                    raw_copy(x, h, way).wait_recv()
                packed_copy(h, way).wait_recv()

        cols = pl.ds(pl.multiple_of(h * d, d), d)
        for r0 in range(0, rows, rows):
            rs = slice(0, rows)
            dq, o = query_block(h, q_own[h], g_own[h], el, rows, 0, count, None)
            out_ref[1, rs, cols] = dq
            out_ref[0, rs, cols] = o
        qb, gb = kv[h, 0, high, :], kv[h, 1, high, :]
        qt[h, :, rows : rows + er] = jnp.transpose(qb)
        gt[h, :, rows : rows + er] = jnp.transpose(gb)
        moved = query_block(h, qb, gb, el + rows, er, hl, k + er, moved_in_r)
        near = key_grads(h, k, k + 128, from_high=True)
        mid = key_grads(h, k + 128, k + 256)
        far = key_grads(h, k + 256, k + 384, own=(half, rows))
        for x in range(2):
            back_r[h, x, 0:128] = near[x].astype(BF)
            back_r[h, x, 128:raw] = mid[x][0 : raw - 128].astype(BF)
            tail = jnp.concatenate([mid[x][raw - 128 :], far[x][0 : hr - 256]], axis=0)
            back_r[h, x, raw:hr] = jnp.where(mask(shared_r, er), tail.astype(BF), moved[x])

        @pl.when(has_right)
        def _():
            back_copy(h, 0).start()

        return carry


    def left_side(h, carry):
        qb, gb = kv[h, 0, low, :], kv[h, 1, low, :]
        qt[h, :, rows + er : rows + er + el] = jnp.transpose(qb)
        gt[h, :, rows + er : rows + er + el] = jnp.transpose(gb)
        moved = query_block(h, qb, gb, 0, el, hl - 256, k, moved_in_l)
        far = key_grads(h, 0, 128, own=(0, half))
        mid = key_grads(h, 128, 256, from_low=True)
        near = key_grads(h, 256, 384, from_low=True)
        for x in range(2):
            head = jnp.concatenate([far[x], mid[x][0 : el - 128]], axis=0)
            back_l[h, x, 0:el] = jnp.where(mask(shared_l, el), head.astype(BF), moved[x])
            back_l[h, x, el:256] = mid[x][el - 128 :].astype(BF)
            back_l[h, x, 256:hl] = near[x].astype(BF)

        @pl.when(has_left)
        def _():
            back_copy(h, 1).start()

        return carry

    lax.fori_loop(0, heads, lambda h, c: left_side(h, right_side(h, c)), 0)

    def own_key_grads(h, carry):
        for i in range(2):
            rs = pl.ds(i * half, half)
            own_kv[h, 0, rs, :], own_kv[h, 1, rs, :] = key_grads(
                h, hl + i * half, hl + (i + 1) * half, from_low=True, from_high=True
            )
        return carry

    lax.fori_loop(0, heads, own_key_grads, 0)

    row_l = (begin[hl : hl + er] < lo) & (jnp.broadcast_to(moved_out_l, (er, 1)) > 0.5)
    row_r = (end[k - el : k] > hi) & (jnp.broadcast_to(moved_out_r, (el, 1)) > 0.5)
    add_l, add_r = mask(shared_l, hr), mask(shared_r, hl)
    tail = rows - el
    for h in range(heads):
        for way in range(2):

            @pl.when(here[way])
            def _(h=h, way=way):
                back_copy(h, way).wait_recv()

        cols = slice(h * d, (h + 1) * d)
        for x in range(2):
            fl = from_left[h, x].astype(F32)
            fr = from_right[h, x].astype(F32)
            out_ref[1 - x, 0:er, cols] = jnp.where(
                row_l, from_left[h, x, raw:hr, :], out_ref[1 - x, 0:er, cols]
            )
            out_ref[1 - x, tail:rows, cols] = jnp.where(
                row_r, from_right[h, x, 0:el, :], out_ref[1 - x, tail:rows, cols]
            )
            own_kv[h, x, 0:hr, :] += jnp.where(add_l, fl, 0.0)
            own_kv[h, x, rows - hl : rows, :] += jnp.where(add_r, fr, 0.0)
            out_ref[2 + x, er:tail, cols] = own_kv[h, x, er:tail, :].astype(BF)
            out_ref[2 + x, 0:er, cols] = jnp.where(
                row_l, fl[0:er], own_kv[h, x, 0:er, :]
            ).astype(BF)
            out_ref[2 + x, tail:rows, cols] = jnp.where(
                row_r, fr[hl - el :], own_kv[h, x, tail:rows, :]
            ).astype(BF)
    for h in range(heads):
        for way in range(2):

            @pl.when(there[way])
            def _(h=h, way=way):
                for x in range(2):
                    raw_copy(x, h, way).wait_send()
                packed_copy(h, way).wait_send()
                back_copy(h, way).wait_send()


def body(queries, keys, values, out_grad, lengths):
    rows, width = queries.shape
    heads = width // D
    n_dp = lax.axis_size("dp")
    count = HALO_L + rows + HALO_R + PAD
    qrows = EDGE_L + rows + EDGE_R
    pairs = qrows * count * heads
    operands = [
        pltpu.with_memory_space_constraint(x, pltpu.MemorySpace.HBM)
        for x in (queries, keys, values, out_grad, lengths.reshape(-1, 128))
    ]
    results = pl.pallas_call(
        functools.partial(kernel, n_dp, rows, heads),
        out_shape=jax.ShapeDtypeStruct((4, rows, width), BF),
        in_specs=[pl.BlockSpec(memory_space=pltpu.MemorySpace.HBM)] * 5,
        out_specs=pl.BlockSpec(memory_space=pltpu.VMEM),
        scratch_shapes=[
            pltpu.VMEM((heads, 2, count, D), BF),
            pltpu.VMEM((heads, rows, D), BF),
            pltpu.VMEM((heads, rows, D), BF),
            pltpu.VMEM((heads, D, qrows), BF),
            pltpu.VMEM((heads, D, qrows), BF),
            pltpu.VMEM((heads, 2, EDGE_L, D), BF),
            pltpu.VMEM((heads, 2, EDGE_R, D), BF),
            pltpu.VMEM((heads, 2, HALO_R, D), BF),
            pltpu.VMEM((heads, 2, HALO_L, D), BF),
            pltpu.VMEM((heads, 2, HALO_R, D), BF),
            pltpu.VMEM((heads, 2, HALO_L, D), BF),
            pltpu.VMEM((qrows, D), F32),
            pltpu.VMEM((8, count), F32),
            pltpu.VMEM((heads, qrows, count), BF),
            pltpu.VMEM((heads, qrows, count), BF),
            pltpu.VMEM((heads, 2, rows, D), F32),
            pltpu.VMEM((lengths.shape[0] // 128, 128), jnp.int32),
            pltpu.SemaphoreType.DMA((heads, 4)),
            pltpu.SemaphoreType.DMA(()),
            pltpu.SemaphoreType.DMA((heads, 3, 2)),
            pltpu.SemaphoreType.DMA((heads, 3, 2)),
            pltpu.SemaphoreType.DMA((heads, 2)),
            pltpu.SemaphoreType.DMA((heads, 2)),
            pltpu.SemaphoreType.REGULAR,
        ],
        compiler_params=pltpu.CompilerParams(
            collective_id=0, has_side_effects=True, vmem_limit_bytes=48 << 20
        ),
        cost_estimate=pl.CostEstimate(
            flops=12 * pairs * D, bytes_accessed=16 * rows * width, transcendentals=pairs
        ),
    )(*operands)
    return tuple(results[x] for x in range(4))


def solution(mesh):
    spec = P("dp", "tensor")
    return jax.shard_map(
        body, mesh=mesh, in_specs=(spec,) * 4 + (P(),), out_specs=(spec,) * 4, check_vma=False
    )
```

```python
import functools
import math

import jax
import jax.numpy as jnp
from jax import lax
from jax.experimental import pallas as pl
from jax.experimental.pallas import tpu as pltpu
from jax.sharding import PartitionSpec as P

D = 128
EDGE_L, EDGE_R = 192, 128
HALO_L, HALO_R = 384, 320
PAD = 64
MESH = pl.DeviceIdType.MESH
LOG2E = 1.4426950408889634
BF = jnp.bfloat16
F32 = jnp.float32


def dot_nt(a, b):
    return lax.dot_general(a, b, (((1,), (1,)), ((), ())), preferred_element_type=F32)


def dot_nn(a, b):
    return jnp.dot(a, b, preferred_element_type=F32)


def row_tables(lens, first, count):
    upper = (
        lax.broadcasted_iota(jnp.int32, (128, 128), 0)
        <= lax.broadcasted_iota(jnp.int32, (128, 128), 1)
    ).astype(F32).astype(BF)
    high = (lens >> 4).astype(F32).astype(BF)
    low = (lens & 15).astype(F32).astype(BF)
    within = 16.0 * dot_nn(high, upper) + dot_nn(low, upper)
    pos = (first - HALO_L + lax.broadcasted_iota(jnp.int32, (count, 128), 0)).astype(F32)
    begin = jnp.zeros((count, 128), F32)
    end = jnp.full((count, 128), 1e9, F32)
    base = jnp.zeros((1, 1), F32)
    for g in range(lens.shape[0]):
        e = within[g : g + 1, :] + base
        base = base + within[g : g + 1, 127:128]
        past = e <= pos
        begin = jnp.maximum(begin, jnp.where(past, e, 0.0))
        end = jnp.minimum(end, jnp.where(past, 1e9, e))
    begin = jnp.max(begin, axis=1, keepdims=True)
    end = jnp.min(end, axis=1, keepdims=True)
    return jnp.where(pos[:, :1] < 0.0, -1.0, begin), end


def kernel(
    n_dp, rows, heads,
    q_hbm, k_hbm, v_hbm, g_hbm, len_hbm,
    out_ref,
    kv, q_own, g_own, qt, gt, packed_r, packed_l, back_r, back_l, from_left, from_right,
    idc, idr, p_s, ds_s, own_kv, len_ref,
    own_sem, len_sem, send1, recv1, send2, recv2, ready,
):
    hl, hr, el, er, d = HALO_L, HALO_R, EDGE_L, EDGE_R, D
    count = hl + rows + hr + PAD
    qrows = el + rows + er
    me = lax.axis_index("dp")
    ten = lax.axis_index("tensor")
    right = lax.rem(me + 1, n_dp)
    left = lax.rem(me + n_dp - 1, n_dp)
    has_left, has_right = me > 0, me < n_dp - 1
    there = (has_right, has_left)
    here = (has_left, has_right)
    raw = hl - el
    assert raw == hr - er

    def remote(src, dst, send, recv, who):
        return pltpu.make_async_remote_copy(
            src_ref=src, dst_ref=dst, send_sem=send, recv_sem=recv,
            device_id=(who, ten), device_id_type=MESH,
        )

    def raw_copy(x, h, way):
        src = pl.ds(rows - raw, raw) if way == 0 else pl.ds(0, raw)
        dst = pl.ds(el, raw) if way == 0 else pl.ds(hl + rows, raw)
        return remote(
            (k_hbm, v_hbm)[x].at[src, pl.ds(h * d, d)], kv.at[h, x, dst, :],
            send1.at[h, x, way], recv1.at[h, x, way], (right, left)[way],
        )

    def packed_copy(h, way):
        dst = pl.ds(0, el) if way == 0 else pl.ds(hl + rows + raw, er)
        return remote(
            (packed_r, packed_l)[way].at[h], kv.at[h, :, dst, :],
            send1.at[h, 2, way], recv1.at[h, 2, way], (right, left)[way],
        )

    def back_copy(h, way):
        return remote(
            (back_r, back_l)[way].at[h], (from_left, from_right)[way].at[h],
            send2.at[h, way], recv2.at[h, way], (right, left)[way],
        )

    def own_copy(x, h):
        mid = pl.ds(hl, rows)
        dst = (q_own.at[h], kv.at[h, 0, mid, :], kv.at[h, 1, mid, :], g_own.at[h])[x]
        src = (q_hbm, k_hbm, v_hbm, g_hbm)[x]
        return pltpu.make_async_copy(src.at[:, pl.ds(h * d, d)], dst, own_sem.at[h, x])

    barrier = pltpu.get_barrier_semaphore()

    @pl.when(has_left)
    def _():
        pl.semaphore_signal(barrier, inc=1, device_id=(left, ten), device_id_type=MESH)

    len_copy = pltpu.make_async_copy(len_hbm, len_ref, len_sem)
    len_copy.start()
    for h in range(heads):
        for x in range(4):
            own_copy(x, h).start()
    @pl.when(has_right)
    def _():
        pl.semaphore_wait(barrier, 1)
        pl.semaphore_signal(ready, inc=1, device_id=(right, ten), device_id_type=MESH)
        for x in range(2):
            raw_copy(x, 0, 0).start()

    @pl.when(jnp.logical_not(has_left))
    def _():
        kv[:, :, 0:hl, :] = jnp.zeros((heads, 2, hl, d), BF)
        from_left[...] = jnp.zeros((heads, 2, hr, d), BF)

    @pl.when(jnp.logical_not(has_right))
    def _():
        kv[:, :, hl + rows : hl + rows + hr, :] = jnp.zeros((heads, 2, hr, d), BF)
        from_right[...] = jnp.zeros((heads, 2, hl, d), BF)


    kv[:, :, count - PAD :, :] = jnp.zeros((heads, 2, PAD, d), BF)
    first = me * rows
    len_copy.wait()
    begin, end = row_tables(len_ref[...], first, count)
    wide = jnp.broadcast_to(begin, (count, d))
    idc[...] = wide[hl - el : hl + rows + er]
    idr[...] = jnp.transpose(wide)[:8, :]
    lo = first.astype(F32)
    hi = (first + rows).astype(F32)
    b0, e0 = begin[hl : hl + 1], end[hl : hl + 1]
    spans_l = b0 < lo
    keep_l = spans_l & (e0 - lo > er)
    moved_in_l = jnp.where(keep_l & (lo - b0 <= el), 1.0, 0.0)
    shared_l = jnp.where(keep_l & (lo - b0 > el), 1.0, 0.0)
    b1, e1 = begin[hl + rows - 1 : hl + rows], end[hl + rows - 1 : hl + rows]
    spans_r = e1 > hi
    moved_in_r = jnp.where(spans_r & (e1 - hi <= er), 1.0, 0.0)
    far_r = spans_r & (e1 - hi > er)
    moved_out_r = jnp.where(far_r & (hi - b1 <= el), 1.0, 0.0)
    shared_r = jnp.where(far_r & (hi - b1 > el), 1.0, 0.0)
    moved_out_l = jnp.where(spans_l & (e0 - lo <= er), 1.0, 0.0)

    def mask(flag, n):
        return jnp.broadcast_to(flag, (n, d)) > 0.5


    for h in range(heads):
        for x in range(4):
            own_copy(x, h).wait()
        for x, own in ((0, q_own), (1, g_own)):
            packed_r[h, x] = jnp.where(
                mask(shared_r, el), kv[h, x, rows : rows + el, :], own[h, rows - el : rows, :]
            )
            packed_l[h, x] = jnp.where(
                mask(shared_l, er), kv[h, x, hl + raw : hl + raw + er, :], own[h, 0:er, :]
            )

        @pl.when(has_right)
        def _(h=h):
            packed_copy(h, 0).start()
            if h + 1 < heads:
                for x in range(2):
                    raw_copy(x, h + 1, 0).start()

    @pl.when(has_left)
    def _():
        pl.semaphore_wait(ready, 1)
        for h in range(heads):
            for x in range(2):
                raw_copy(x, h, 1).start()
            packed_copy(h, 1).start()

    for h in range(heads):
        qt[h, :, 0:rows] = jnp.transpose(q_own[h])
        gt[h, :, 0:rows] = jnp.transpose(g_own[h])

    factor = 1.0 / math.sqrt(d)
    half = rows // 2
    k = hl + rows
    low, high = slice(0, el), slice(k + raw, k + raw + er)

    def query_block(h, qb, gb, r0, n, k0, k1, valid):
        kb, vb = kv[h, 0, k0:k1, :], kv[h, 1, k0:k1, :]
        s = dot_nt(qb, kb) * (factor * LOG2E)
        s = jnp.where(idc[r0 : r0 + n, :1] == idr[:1, k0:k1], s, -1e30)
        top = jnp.max(s, axis=1, keepdims=True)
        w = jnp.exp2(s - top)
        total = jnp.sum(w, axis=1, keepdims=True)
        probs = w * ((1.0 if valid is None else valid) / total)
        p = probs.astype(BF)
        o = dot_nn(p, vb).astype(BF)
        p_s[h, r0 : r0 + n, k0:k1] = p
        gp = dot_nt(gb, vb)
        centre = jnp.sum(gb.astype(F32) * o.astype(F32), axis=1, keepdims=True)
        ds = (probs * (gp - centre)).astype(BF)
        ds_s[h, r0 : r0 + n, k0:k1] = ds
        return (dot_nn(ds, kb) * factor).astype(BF), o

    def key_grads(h, c0, c1, own=(0, rows), from_low=False, from_high=False, kind=BF):
        cs = slice(c0, c1)
        rs = slice(el + own[0], el + own[1])
        dk = dot_nn(qt[h, :, own[0] : own[1]], ds_s[h, rs, cs])
        dv = dot_nn(gt[h, :, own[0] : own[1]], p_s[h, rs, cs])
        if from_high:
            rs = slice(el + rows, qrows)
            dk += dot_nn(qt[h, :, rows : rows + er], ds_s[h, rs, cs])
            dv += dot_nn(gt[h, :, rows : rows + er], p_s[h, rs, cs])
        if from_low:
            rs, ts = slice(0, el), slice(rows + er, rows + er + el)
            dk += dot_nn(qt[h, :, ts], ds_s[h, rs, cs])
            dv += dot_nn(gt[h, :, ts], p_s[h, rs, cs])
        return jnp.transpose((dk * factor).astype(kind)), jnp.transpose(dv.astype(kind))

    def right_side(h, carry):
        for way in range(2):

            @pl.when(here[way])
            def _(way=way):
                for x in range(2):
                    raw_copy(x, h, way).wait_recv()
                packed_copy(h, way).wait_recv()

        cols = pl.ds(pl.multiple_of(h * d, d), d)
        for r0 in range(0, rows, rows):
            rs = slice(0, rows)
            dq, o = query_block(h, q_own[h], g_own[h], el, rows, 0, count, None)
            out_ref[1, rs, cols] = dq
            out_ref[0, rs, cols] = o
        qb, gb = kv[h, 0, high, :], kv[h, 1, high, :]
        qt[h, :, rows : rows + er] = jnp.transpose(qb)
        gt[h, :, rows : rows + er] = jnp.transpose(gb)
        moved = query_block(h, qb, gb, el + rows, er, hl, k + er, moved_in_r)
        near = key_grads(h, k, k + 128, from_high=True)
        mid = key_grads(h, k + 128, k + 256)
        far = key_grads(h, k + 256, k + 384, own=(half, rows))
        for x in range(2):
            back_r[h, x, 0:128] = near[x]
            back_r[h, x, 128:raw] = mid[x][0 : raw - 128]
            tail = jnp.concatenate([mid[x][raw - 128 :], far[x][0 : hr - 256]], axis=0)
            back_r[h, x, raw:hr] = jnp.where(mask(shared_r, er), tail, moved[x])

        @pl.when(has_right)
        def _():
            back_copy(h, 0).start()

        return carry


    def left_side(h, carry):
        qb, gb = kv[h, 0, low, :], kv[h, 1, low, :]
        qt[h, :, rows + er : rows + er + el] = jnp.transpose(qb)
        gt[h, :, rows + er : rows + er + el] = jnp.transpose(gb)
        moved = query_block(h, qb, gb, 0, el, hl - 256, k, moved_in_l)
        far = key_grads(h, 0, 128, own=(0, half))
        mid = key_grads(h, 128, 256, from_low=True)
        near = key_grads(h, 256, 384, from_low=True)
        for x in range(2):
            head = jnp.concatenate([far[x], mid[x][0 : el - 128]], axis=0)
            back_l[h, x, 0:el] = jnp.where(mask(shared_l, el), head, moved[x])
            back_l[h, x, el:256] = mid[x][el - 128 :]
            back_l[h, x, 256:hl] = near[x]

        @pl.when(has_left)
        def _():
            back_copy(h, 1).start()

        return carry

    lax.fori_loop(0, heads, lambda h, c: left_side(h, right_side(h, c)), 0)

    def own_key_grads(h, carry):
        for i in range(2):
            rs = pl.ds(i * half, half)
            own_kv[h, 0, rs, :], own_kv[h, 1, rs, :] = key_grads(
                h, hl + i * half, hl + (i + 1) * half, from_low=True, from_high=True, kind=F32
            )
        return carry

    lax.fori_loop(0, heads, own_key_grads, 0)

    row_l = (begin[hl : hl + er] < lo) & (jnp.broadcast_to(moved_out_l, (er, 1)) > 0.5)
    row_r = (end[k - el : k] > hi) & (jnp.broadcast_to(moved_out_r, (el, 1)) > 0.5)
    add_l, add_r = mask(shared_l, hr), mask(shared_r, hl)
    tail = rows - el
    for h in range(heads):
        for way in range(2):

            @pl.when(here[way])
            def _(h=h, way=way):
                back_copy(h, way).wait_recv()

        cols = slice(h * d, (h + 1) * d)
        for x in range(2):
            fl = from_left[h, x].astype(F32)
            fr = from_right[h, x].astype(F32)
            out_ref[1 - x, 0:er, cols] = jnp.where(
                row_l, from_left[h, x, raw:hr, :], out_ref[1 - x, 0:er, cols]
            )
            out_ref[1 - x, tail:rows, cols] = jnp.where(
                row_r, from_right[h, x, 0:el, :], out_ref[1 - x, tail:rows, cols]
            )
            own_kv[h, x, 0:hr, :] += jnp.where(add_l, fl, 0.0)
            own_kv[h, x, rows - hl : rows, :] += jnp.where(add_r, fr, 0.0)
            out_ref[2 + x, er:tail, cols] = own_kv[h, x, er:tail, :].astype(BF)
            out_ref[2 + x, 0:er, cols] = jnp.where(
                row_l, fl[0:er], own_kv[h, x, 0:er, :]
            ).astype(BF)
            out_ref[2 + x, tail:rows, cols] = jnp.where(
                row_r, fr[hl - el :], own_kv[h, x, tail:rows, :]
            ).astype(BF)
    for h in range(heads):
        for way in range(2):

            @pl.when(there[way])
            def _(h=h, way=way):
                for x in range(2):
                    raw_copy(x, h, way).wait_send()
                packed_copy(h, way).wait_send()
                back_copy(h, way).wait_send()


def body(queries, keys, values, out_grad, lengths):
    rows, width = queries.shape
    heads = width // D
    n_dp = lax.axis_size("dp")
    count = HALO_L + rows + HALO_R + PAD
    qrows = EDGE_L + rows + EDGE_R
    pairs = qrows * count * heads
    operands = [
        pltpu.with_memory_space_constraint(x, pltpu.MemorySpace.HBM)
        for x in (queries, keys, values, out_grad, lengths.reshape(-1, 128))
    ]
    results = pl.pallas_call(
        functools.partial(kernel, n_dp, rows, heads),
        out_shape=jax.ShapeDtypeStruct((4, rows, width), BF),
        in_specs=[pl.BlockSpec(memory_space=pltpu.MemorySpace.HBM)] * 5,
        out_specs=pl.BlockSpec(memory_space=pltpu.VMEM),
        scratch_shapes=[
            pltpu.VMEM((heads, 2, count, D), BF),
            pltpu.VMEM((heads, rows, D), BF),
            pltpu.VMEM((heads, rows, D), BF),
            pltpu.VMEM((heads, D, qrows), BF),
            pltpu.VMEM((heads, D, qrows), BF),
            pltpu.VMEM((heads, 2, EDGE_L, D), BF),
            pltpu.VMEM((heads, 2, EDGE_R, D), BF),
            pltpu.VMEM((heads, 2, HALO_R, D), BF),
            pltpu.VMEM((heads, 2, HALO_L, D), BF),
            pltpu.VMEM((heads, 2, HALO_R, D), BF),
            pltpu.VMEM((heads, 2, HALO_L, D), BF),
            pltpu.VMEM((qrows, D), F32),
            pltpu.VMEM((8, count), F32),
            pltpu.VMEM((heads, qrows, count), BF),
            pltpu.VMEM((heads, qrows, count), BF),
            pltpu.VMEM((heads, 2, rows, D), F32),
            pltpu.VMEM((lengths.shape[0] // 128, 128), jnp.int32),
            pltpu.SemaphoreType.DMA((heads, 4)),
            pltpu.SemaphoreType.DMA(()),
            pltpu.SemaphoreType.DMA((heads, 3, 2)),
            pltpu.SemaphoreType.DMA((heads, 3, 2)),
            pltpu.SemaphoreType.DMA((heads, 2)),
            pltpu.SemaphoreType.DMA((heads, 2)),
            pltpu.SemaphoreType.REGULAR,
        ],
        compiler_params=pltpu.CompilerParams(
            collective_id=0, has_side_effects=True, vmem_limit_bytes=48 << 20
        ),
        cost_estimate=pl.CostEstimate(
            flops=12 * pairs * D, bytes_accessed=16 * rows * width, transcendentals=pairs
        ),
    )(*operands)
    return tuple(results[x] for x in range(4))


def solution(mesh):
    spec = P("dp", "tensor")
    return jax.shard_map(
        body, mesh=mesh, in_specs=(spec,) * 4 + (P(),), out_specs=(spec,) * 4, check_vma=False
    )
```
